32 devices in a mesh: seq: 32 (over z, y, x, core).
Axes of the slice: x: 2, y: 2, z: 4, core: 2. Of those that a mesh axis runs over, the one named last changes fastest.
Arguments:
- tokens: bfloat16 [32768, 1024], P('seq'), may hold values from -16 to 16
- w_query: bfloat16 [1024, 1024], replicated, may hold values from -0.1875 to 0.1875
- w_key: bfloat16 [1024, 1024], replicated, may hold values from -0.1875 to 0.1875
- w_value: bfloat16 [1024, 1024], replicated, may hold values from -0.1875 to 0.1875
- w_out: bfloat16 [1024, 1024], replicated, may hold values from -0.1875 to 0.1875
- rand_blocks: int32 [512, 3], P('seq'), may hold values from 0 to 511, as said below
- global_pos: int32 [128], replicated, may hold values from 0 to 32767, as said below
Outputs:
- mixed: bfloat16 [32768, 1024], P('seq')
The draws below stay inside these ranges and needn't reach their ends.
Inputs may be any that keep to these rules, and one draw needn't show every extreme that they name: `rand_blocks`: the entries of a row differ, and none is the row's block or a block next to it. All entries lie on the row's own device (blocks of 16 per device, contiguous), except that for each device and each offset o of -3 to -1 and 1 to 3 for which a device o away exists, exactly one row of the device has its last entry on the device o away. `global_pos`: distinct and increasing.
All inputs are finite; a program needn't handle non-finite values.
Results may differ from the reference program's by a relative error of at most 0.003.
The reference program's roundings to bfloat16 on the way count: a program that leaves them out, or rounds other values in their place, can miss the bound.
Values may be sent and summed in bfloat16 or wider, within the bound.
A program may use at most 192 MiB of HBM per device.

```python
import math
import jax
import jax.numpy as jnp
from jax import lax

D = 1024
HEADS = 16
HD = 64
BLK = 64
RAND = 3
NG = 128
FAR = 3
TOK_DEV = 1024
NBLOCKS = 512
TOKENS = 32768
N_SEQ = 32


def draw_tokens(key, part):
    first_key = jax.random.fold_in(key, 0)
    values = jnp.clip(jax.random.normal(first_key, (TOKENS, D), jnp.float32), -6.0, 6.0)
    return values.astype(jnp.bfloat16)


def draw_rand_blocks(key, part):
    block_count = TOK_DEV // BLK
    seq_count = NBLOCKS // block_count
    first_key, second_key, third_key = jax.random.split(key, 3)
    local_index = jnp.arange(NBLOCKS, dtype=jnp.int32) % block_count
    candidates = jnp.arange(block_count, dtype=jnp.int32)
    scores = jax.random.randint(first_key, (NBLOCKS, block_count), 0, 65536) * block_count + candidates[None, :]
    allowed = jnp.abs(candidates[None, :] - local_index[:, None]) > 1
    scores = jnp.where(allowed, scores, -1)
    top_values, chosen = lax.top_k(scores, RAND)
    device_of_row = jnp.arange(NBLOCKS, dtype=jnp.int32) // block_count
    chosen = chosen.astype(jnp.int32) + device_of_row[:, None] * block_count
    device_keys = jax.random.split(second_key, seq_count)
    chosen_rows = jax.vmap(lambda item_key: jax.random.permutation(item_key, block_count))(device_keys)[:, :2 * FAR]
    chosen_rows = chosen_rows.astype(jnp.int32)
    offsets = jnp.concatenate([jnp.arange(-FAR, 0), jnp.arange(1, FAR + 1)]).astype(jnp.int32)
    device_ids = jnp.arange(seq_count, dtype=jnp.int32)[:, None]
    target = device_ids + offsets[None, :]
    in_range = (target >= 0) & (target < seq_count)
    far_local = jax.random.randint(third_key, (seq_count, 2 * FAR), 1, block_count - 1).astype(jnp.int32)
    row_ids = (device_ids * block_count + chosen_rows).reshape(-1)
    old_last = chosen[row_ids, RAND - 1].reshape(seq_count, 2 * FAR)
    new_last = jnp.where(in_range, target * block_count + far_local, old_last).reshape(-1)
    last_column = chosen[:, RAND - 1].at[row_ids].set(new_last)
    return chosen.at[:, RAND - 1].set(last_column).astype(jnp.int32)


def draw_global_pos(key, part):
    shuffled = jax.random.permutation(key, TOKENS)[:NG]
    return jnp.sort(shuffled).astype(jnp.int32)


def bell_draw(rng, dims, deviation, limit, kind=jnp.bfloat16):
    array = deviation * jax.random.normal(rng, dims, jnp.float32)
    return jnp.clip(array, min=-limit, max=limit).astype(kind)


def setup_inputs(seed: int = 0) -> dict:
    key_of = jax.random.split(jax.random.key(seed), 8)
    tokens = draw_tokens(jax.random.fold_in(key_of[7], 71), 0)
    w_query = bell_draw(key_of[1], (D, D), D ** -0.5, 0.1875)
    w_key = bell_draw(key_of[2], (D, D), D ** -0.5, 0.1875)
    w_value = bell_draw(key_of[3], (D, D), D ** -0.5, 0.1875)
    w_out = bell_draw(key_of[4], (D, D), D ** -0.5, 0.1875)
    rand_blocks = draw_rand_blocks(jax.random.fold_in(key_of[7], 71), 0)
    global_pos = draw_global_pos(jax.random.fold_in(key_of[7], 71), 0)
    return dict(tokens=tokens, w_query=w_query, w_key=w_key, w_value=w_value, w_out=w_out, rand_blocks=rand_blocks, global_pos=global_pos)


def reference(tokens, w_query, w_key, w_value, w_out, rand_blocks, global_pos):
    queries = jnp.dot(tokens, w_query, preferred_element_type=jnp.float32).astype(jnp.bfloat16)
    keys = jnp.dot(tokens, w_key, preferred_element_type=jnp.float32).astype(jnp.bfloat16)
    values = jnp.dot(tokens, w_value, preferred_element_type=jnp.float32).astype(jnp.bfloat16)
    block_count = tokens.shape[0] // BLK
    query_blocks = queries.reshape(block_count, BLK, HEADS, HD)
    key_blocks = keys.reshape(block_count, BLK, HEADS, HD)
    value_blocks = values.reshape(block_count, BLK, HEADS, HD)
    global_keys = keys[global_pos].reshape(NG, HEADS, HD).astype(jnp.float32)
    global_values = values[global_pos].reshape(NG, HEADS, HD).astype(jnp.float32)
    score_scale = 1.0 / math.sqrt(HD)
    group_size = math.gcd(block_count, max(1, 512 // BLK))

    def attend_group(start):
        block_ids = start + jnp.arange(group_size, dtype=jnp.int32)
        window = jnp.stack([block_ids - 1, block_ids, block_ids + 1], axis=1)
        window_ok = (window >= 0) & (window < block_count)
        chosen = lax.dynamic_slice_in_dim(rand_blocks, start, group_size, 0).astype(jnp.int32)
        index_set = jnp.concatenate([jnp.clip(window, 0, block_count - 1), chosen], axis=1)
        valid_set = jnp.concatenate([window_ok, jnp.ones((group_size, RAND), bool)], axis=1)
        key_heads = key_blocks[index_set].reshape(group_size, -1, HEADS, HD).astype(jnp.float32)
        value_heads = value_blocks[index_set].reshape(group_size, -1, HEADS, HD).astype(jnp.float32)
        key_valid = jnp.repeat(valid_set, BLK, axis=1)
        query_group = lax.dynamic_slice_in_dim(query_blocks, start, group_size, 0).astype(jnp.float32)
        local_scores = jnp.einsum('gqhd,gkhd->ghqk', query_group, key_heads) * score_scale
        local_scores = jnp.where(key_valid[:, None, None, :], local_scores, -1e+30)
        global_scores = jnp.einsum('gqhd,khd->ghqk', query_group, global_keys) * score_scale
        all_scores = jnp.concatenate([local_scores, global_scores], axis=-1)
        top_score = lax.optimization_barrier(jnp.max(all_scores, axis=-1, keepdims=True))
        exps = jnp.exp(all_scores - top_score)
        weights = lax.optimization_barrier((exps / lax.optimization_barrier(jnp.sum(exps, axis=-1, keepdims=True))).astype(jnp.bfloat16))
        weights = weights.astype(jnp.float32)
        split_at = key_heads.shape[1]
        result = jnp.einsum('ghqk,gkhd->gqhd', weights[..., :split_at], value_heads)
        result = result + jnp.einsum('ghqk,khd->gqhd', weights[..., split_at:], global_values)
        return result.astype(jnp.bfloat16)
    starts = jnp.arange(0, block_count, group_size, dtype=jnp.int32)
    sparse = lax.map(attend_group, starts).reshape(-1, D)
    global_queries = queries[global_pos].reshape(NG, HEADS, HD).astype(jnp.float32)
    key_shards = keys.reshape(N_SEQ, -1, HEADS, HD)
    value_shards = values.reshape(N_SEQ, -1, HEADS, HD)

    def shard_sums(shard):
        shard_keys = key_shards[shard].astype(jnp.float32)
        shard_values = value_shards[shard].astype(jnp.float32)
        gscore = jnp.einsum('qhd,khd->hqk', global_queries, shard_keys) * score_scale
        speak = lax.optimization_barrier(jnp.max(gscore, axis=-1))
        gexp = jnp.exp(gscore - speak[:, :, None])
        stotal = lax.optimization_barrier(jnp.sum(gexp, axis=-1))
        rounded = lax.optimization_barrier(gexp.astype(jnp.bfloat16)).astype(jnp.float32)
        snum = jnp.einsum('hqk,khd->qhd', rounded, shard_values)
        return (speak, stotal, snum)
    shard_ids = jnp.arange(N_SEQ, dtype=jnp.int32)
    peaks, totals, numerators = lax.map(shard_sums, shard_ids)
    peak_score = lax.optimization_barrier(jnp.max(peaks, axis=0))
    factors = jnp.exp(peaks - peak_score[None])
    gtotal = lax.optimization_barrier(jnp.sum(totals * factors, axis=0))
    gnum = lax.optimization_barrier(jnp.sum(numerators * jnp.transpose(factors, (0, 2, 1))[:, :, :, None], axis=0))
    gout = (gnum / jnp.transpose(gtotal)[:, :, None]).reshape(NG, D).astype(jnp.bfloat16)
    attended = sparse.at[global_pos].set(gout)
    return jnp.dot(attended, w_out, preferred_element_type=jnp.float32).astype(jnp.bfloat16)
```

```python
import functools
import math

import jax
import jax.numpy as jnp
from jax import lax
from jax.experimental import pallas as pl
from jax.experimental.pallas import tpu as pltpu
from jax.sharding import PartitionSpec as P

HEADS = 16
HD = 64
BLK = 64
RAND = 3
NG = 128
FAR = 3
OFFSETS = tuple(range(-FAR, 0)) + tuple(range(1, FAR + 1))
NFAR = len(OFFSETS)
LANES = 128
EXP_SCALE = math.log2(math.e) / math.sqrt(HD)
SCORE_SCALE = 1.0 / math.sqrt(HD)
MESH = pl.DeviceIdType.MESH
BF = jnp.bfloat16
F32 = jnp.float32
NT = (((1,), (1,)), ((), ()))


def attention(
    n,
    tok_hbm, wq_hbm, wk_hbm, wv_hbm, rbv_ref, grow_ref, rb_ref,
    sp, gout, place,
    xt, wq, wk, wv, q, kv, xg, gq, gf, sel, far, land,
    req_out, reqin, order, rs_out, rs_in, ag, cn_out, cn_in, cs_out, cs_in, ag2,
    sc, top, ex, inv,
    load_sem, req_s, req_r, edge_s, edge_r,
    rs_s, rs_r, ag_s, ag_r, cn_s, cn_r, cs_s, cs_r, ag2_s, ag2_r,
):
    tok_dev, width = tok_hbm.shape
    nblk = tok_dev // BLK
    me = lax.axis_index("seq")
    _, rb, cb = ag.shape
    ncg = width // cb
    hpb = cb // HD
    pairs = width // LANES
    right0 = nblk + 1
    far0 = nblk + 2
    glob0 = far0 + NFAR
    gblk = NG // BLK

    loads = [
        pltpu.make_async_copy(src, dst, load_sem.at[i])
        for i, (src, dst) in enumerate(
            ((tok_hbm, xt), (wk_hbm, wk), (wv_hbm, wv), (wq_hbm, wq))
        )
    ]
    for cp in loads:
        cp.start()

    kv[0] = jnp.zeros(kv.shape[1:], BF)
    kv[right0] = jnp.zeros(kv.shape[1:], BF)
    reqin[...] = jnp.zeros(reqin.shape, jnp.int32)
    base = rbv_ref[RAND - 1:RAND, :] - me * nblk
    for i, o in enumerate(OFFSETS):
        loc = base - o * nblk
        loc = jnp.where((loc >= 0) & (loc < nblk), loc, 0)
        want = jnp.sum(loc, axis=1, keepdims=True)
        req_out[i] = jnp.broadcast_to(want, (8, LANES))

    barrier = pltpu.get_barrier_semaphore()

    def greet(o, c):
        pl.semaphore_signal(
            barrier, inc=1, device_id=(lax.rem(me + o, n),), device_id_type=MESH
        )
        return c

    lax.fori_loop(1, n, greet, 0)
    pl.semaphore_wait(barrier, n - 1)

    def to_all(src, dst, s_sem, r_sem):
        def one(o, c):
            peer = lax.rem(me + o, n)
            pltpu.make_async_remote_copy(
                src_ref=src(peer), dst_ref=dst.at[me], send_sem=s_sem, recv_sem=r_sem,
                device_id=(peer,), device_id_type=MESH,
            ).start()
            return c

        lax.fori_loop(1, n, one, 0)

    def wait_bytes(buf, sem):
        part = buf.at[pl.ds(0, n - 1)]
        pltpu.make_async_copy(part, part, sem).wait()

    def req_copy(i):
        return pltpu.make_async_remote_copy(
            src_ref=req_out.at[i], dst_ref=reqin.at[i], send_sem=req_s.at[i],
            recv_sem=req_r.at[i], device_id=(me + OFFSETS[i],), device_id_type=MESH,
        )

    def far_copy(i):
        return pltpu.make_async_remote_copy(
            src_ref=far.at[i], dst_ref=land.at[2 + i],
            send_sem=edge_s.at[2 + i], recv_sem=edge_r.at[2 + i],
            device_id=(me - OFFSETS[i],), device_id_type=MESH,
        )

    def halo_copy(side):
        src, dst, dev = (1, 1, me - 1) if side == 0 else (nblk, 0, me + 1)
        return pltpu.make_async_remote_copy(
            src_ref=kv.at[src], dst_ref=land.at[dst],
            send_sem=edge_s.at[side], recv_sem=edge_r.at[side],
            device_id=(dev,), device_id_type=MESH,
        )

    def exists(o):
        return me + o >= 0 if o < 0 else me + o < n

    for i, o in enumerate(OFFSETS):
        @pl.when(exists(o))
        def _():
            req_copy(i).start()

    diag = lax.broadcasted_iota(jnp.int32, (NG, NG), 0) == lax.broadcasted_iota(
        jnp.int32, (NG, NG), 1
    )
    gcol = jnp.sum(
        jnp.where(diag, (grow_ref[...] - me * tok_dev).astype(F32), 0.0), axis=1, keepdims=True
    )
    hit = gcol == lax.broadcasted_iota(jnp.int32, (NG, tok_dev), 1).astype(F32)
    sel[...] = jnp.where(hit, 1.0, 0.0).astype(BF)

    loads[0].wait()
    picked = jnp.dot(sel[...], xt[...], preferred_element_type=F32)
    if rb % 16 == 0:
        picked = picked.astype(BF)
        for d in range(n):
            r, c = (d // ncg) * rb, (d % ncg) * cb
            rs_out[d] = picked[r:r + rb, c:c + cb]
    else:
        gf[...] = picked
        for d in range(n):
            r, c = (d // ncg) * rb, (d % ncg) * cb
            rs_out[d] = gf[r:r + rb, c:c + cb].astype(BF)
    to_all(lambda p: rs_out.at[p], rs_in, rs_s, rs_r)

    def project(w, put, step):
        def one(c, carry):
            a = pl.multiple_of(c * step, step)
            val = jnp.dot(
                xt[pl.ds(a, step)], w[...], preferred_element_type=F32
            ).astype(BF)
            for p in range(pairs):
                put(c * (step // BLK), p, val[:, p * LANES:(p + 1) * LANES].reshape(
                    step // BLK, BLK, LANES
                ))
            return carry

        lax.fori_loop(0, tok_dev // step, one, 0)

    step = 512

    def put_kv(which):
        def put(b, p, x):
            kv[pl.ds(1 + b, step // BLK), which, p] = x

        return put

    def put_q(b, p, x):
        q[pl.ds(b, step // BLK), p] = x

    loads[1].wait()
    project(wk, put_kv(0), step)

    rs_in[me] = rs_out[me]
    wait_bytes(rs_in, rs_r)
    ag[me] = jnp.sum(rs_in[...].astype(F32), axis=0).astype(BF)
    to_all(lambda p: ag.at[me], ag, ag_s, ag_r)

    loads[2].wait()
    project(wv, put_kv(1), step)

    for side, o in ((0, -1), (1, 1)):
        @pl.when(exists(o))
        def _():
            halo_copy(side).start()
    for i, o in enumerate(OFFSETS):
        @pl.when(exists(-o))
        def _():
            req_copy(i).wait_recv()
    for i, o in enumerate(OFFSETS):
        far[i] = kv[1 + jnp.minimum(jnp.maximum(reqin[i, 0, 0], 0), nblk - 1)]

        @pl.when(exists(-o))
        def _():
            far_copy(i).start()

    loads[3].wait()
    project(wq, put_q, step)

    lates = []
    for b in range(1, nblk - 1):
        r = rb_ref[RAND - 1, b] - me * nblk
        lates.append(jnp.where((r >= 0) & (r < nblk), 0, 1))
    early = nblk - 2 - sum(lates)
    seen = jnp.int32(0)
    spots = []
    for b in range(1, nblk - 1):
        late = lates[b - 1]
        spots.append(jnp.where(late == 1, early + seen, b - 1 - seen))
        seen = seen + late
        place[b] = spots[b - 1]
    for t in range(nblk - 2):
        order[t] = sum(jnp.where(spots[b - 1] == t, b, 0) for b in range(1, nblk - 1))
    place[0] = nblk - 2
    place[nblk - 1] = nblk - 1

    wait_bytes(ag, ag_r)
    for d in range(n):
        r, c = (d // ncg) * rb, (d % ncg) * cb
        if rb % 16 == 0:
            xg[r:r + rb, c:c + cb] = ag[d]
        else:
            gf[r:r + rb, c:c + cb] = ag[d].astype(F32)
    if rb % 16:
        xg[...] = gf[...].astype(BF)

    for which, w in ((2, wq), (0, wk), (1, wv)):
        val = jnp.dot(xg[...], w[...], preferred_element_type=F32).astype(BF)
        for p in range(pairs):
            x = val[:, p * LANES:(p + 1) * LANES]
            if which == 2:
                gq[p] = x
            else:
                kv[glob0:glob0 + gblk, which, p] = x.reshape(gblk, BLK, LANES)

    lane = lax.broadcasted_iota(jnp.int32, (1, LANES), 1)
    islo = lane < HD
    halves = (jnp.where(islo, 1.0, 0.0).astype(BF), jnp.where(islo, 0.0, 1.0).astype(BF))
    lane_f = lax.broadcasted_iota(jnp.int32, (1, LANES), 1)

    def stacked(x):
        return jnp.concatenate([x * m for m in halves], axis=0)

    def with_ones(x):
        return jnp.concatenate([x, jnp.ones(x.shape, BF)], axis=1)

    per = cb // LANES

    def global_part(cg, carry):
        nums, stat = [], jnp.zeros((NG, LANES), F32)
        for j in range(per):
            p = cg * per + j
            s = lax.dot_general(
                stacked(gq[p]), kv[1:1 + nblk, 0, p].reshape(tok_dev, LANES), NT,
                preferred_element_type=F32,
            )
            m = jnp.max(s, axis=-1, keepdims=True)
            e = jnp.exp2((s - m) * EXP_SCALE).astype(BF)
            x = jnp.dot(
                e, with_ones(kv[1:1 + nblk, 1, p].reshape(tok_dev, LANES)),
                preferred_element_type=F32,
            )
            nums.append(jnp.where(islo, x[:NG, :LANES], x[NG:, :LANES]).astype(BF))
            m = m * SCORE_SCALE
            for h in range(2):
                rows = slice(h * NG, (h + 1) * NG)
                stat = jnp.where(lane_f == 2 * j + h, m[rows], stat)
                stat = jnp.where(lane_f == hpb + 2 * j + h, x[rows, LANES:], stat)
        num = jnp.concatenate(nums, axis=1) if per > 1 else nums[0]
        for rg in range(NG // rb):
            d = rg * ncg + cg
            cn_out[d] = num[rg * rb:(rg + 1) * rb]
            cs_out[d] = stat[rg * rb:(rg + 1) * rb]
        return carry

    lax.fori_loop(0, ncg, global_part, 0)
    to_all(lambda p: cs_out.at[p], cs_in, cs_s, cs_r)
    to_all(lambda p: cn_out.at[p], cn_in, cn_s, cn_r)

    def choose(b):
        picks = []
        for r in range(RAND):
            rel = rb_ref[r, b] - me * nblk
            dev = lax.div(rel + FAR * nblk, nblk)
            slot = jnp.where(dev < FAR, dev, dev - 1)
            pick = jnp.where(dev == FAR, rel + 1, far0 + slot)
            picks.append(jnp.minimum(jnp.maximum(pick, 0), far0 + NFAR - 1))
        return picks

    def rows_of(which, p, b, picks):
        return jnp.concatenate(
            [kv[b + i, which, p] for i in range(3)]
            + [kv[i, which, p] for i in picks]
            + [kv[glob0 + i, which, p] for i in range(gblk)],
            axis=0,
        )

    half = pairs // 2
    nsub = (3 + RAND) * BLK // LANES + NG // LANES

    def wide(x):
        return jnp.concatenate([x] * nsub, axis=1)

    def scores(g, blk):
        t, b, picks, bias = blk
        for j in range(half):
            p = g * half + j
            s = lax.dot_general(
                stacked(q[b, p]), rows_of(0, p, b, picks), NT, preferred_element_type=F32
            )
            if bias is not None:
                s = s + bias
            sc[g, j] = s
            top[g, j] = jnp.broadcast_to(
                jnp.max(s, axis=-1, keepdims=True), (2 * BLK, LANES)
            )

    def expo(g):
        for j in range(half):
            e = jnp.exp2((sc[g, j] - wide(top[g, j])) * EXP_SCALE)
            ex[g, j] = e
            inv[g, j] = jnp.broadcast_to(
                1.0 / jnp.sum(e, axis=-1, keepdims=True), (2 * BLK, LANES)
            )

    def weigh(g, blk):
        t, b, picks, _ = blk
        for j in range(0, half, 2):
            p = g * half + j
            w = jnp.concatenate(
                [(ex[g, j + i] * wide(inv[g, j + i])).astype(BF) for i in range(2)], axis=0
            )
            x = jnp.dot(
                w,
                jnp.concatenate([rows_of(1, p + i, b, picks) for i in range(2)], axis=1),
                preferred_element_type=F32,
            )
            for i in range(2):
                y = x[i * 2 * BLK:(i + 1) * 2 * BLK, i * LANES:(i + 1) * LANES]
                sp[t, p + i] = jnp.where(islo, y[:BLK], y[BLK:]).astype(BF)

    def attend(before, blocks):
        seq = [before] + blocks
        for i, blk in enumerate(blocks):
            expo(1)
            scores(0, blk)
            weigh(0, seq[i])
            expo(0)
            scores(1, blk)
            weigh(1, seq[i])

    def block_at(t, b, bias=None):
        return t, b, choose(b), bias

    def between():
        cs_in[me] = cs_out[me]
        cn_in[me] = cn_out[me]
        wait_bytes(cs_in, cs_r)
        wait_bytes(cn_in, cn_r)
        peak = jnp.max(cs_in[...], axis=0)
        lane_c = lax.broadcasted_iota(jnp.int32, (1, cb), 1) // HD

        def spread(x, first):
            y = jnp.broadcast_to(x[:, first:first + 1], (rb, cb))
            for j in range(1, hpb):
                y = jnp.where(lane_c == j, x[:, first + j:first + j + 1], y)
            return y

        unroll = 4

        def merge(i, c):
            num, den = c
            for j in range(unroll):
                s = i * unroll + j
                stat = cs_in[s]
                fac = jnp.exp(stat - peak)
                prod = fac * pltpu.roll(stat, LANES - hpb, 1)
                num = num + cn_in[s].astype(F32) * spread(fac, 0)
                den = den + prod
            return num, den

        num, den = lax.fori_loop(
            0, n // unroll, merge, (jnp.zeros((rb, cb), F32), jnp.zeros((rb, LANES), F32))
        )
        ag2[me] = (num / spread(den, 0)).astype(BF)
        to_all(lambda p: ag2.at[me], ag2, ag2_s, ag2_r)

        for side, o, slot in ((0, 1, right0), (1, -1, 0)):
            @pl.when(exists(o))
            def _():
                halo_copy(side).wait_recv()
                kv[slot] = land[1 - side]
        for i, o in enumerate(OFFSETS):
            @pl.when(exists(o))
            def _():
                far_copy(i).wait_recv()
                kv[far0 + i] = land[2 + i]

    def two(i, carry):
        @pl.when(i == nblk // 4)
        def _():
            between()

        prev = jnp.maximum(2 * i - 1, 0)
        attend(
            block_at(prev, order[prev]),
            [block_at(2 * i + j, order[2 * i + j]) for j in range(2)],
        )
        return carry

    lax.fori_loop(0, nblk // 2 - 1, two, 0)
    key_col = lax.broadcasted_iota(jnp.int32, (1, (3 + RAND) * BLK + NG), 1)
    lead = jnp.where(me == 0, BLK, 0)
    tail = jnp.where(me == n - 1, 2 * BLK, 3 * BLK)
    first = jnp.where(key_col < lead, -1e30, 0.0)
    last = jnp.where((key_col >= tail) & (key_col < 3 * BLK), -1e30, 0.0)
    end = block_at(nblk - 1, nblk - 1, last)
    attend(block_at(nblk - 3, order[nblk - 3]), [block_at(nblk - 2, 0, first), end])
    expo(1)
    weigh(0, end)
    weigh(1, end)

    wait_bytes(ag2, ag2_r)
    for d in range(n):
        r, c = (d // ncg) * rb, (d % ncg) * cb
        if rb % 16 == 0:
            gout[r:r + rb, c:c + cb] = ag2[d]
        else:
            gf[r:r + rb, c:c + cb] = ag2[d].astype(F32)
    if rb % 16:
        gout[...] = gf[...].astype(BF)

    for i, o in enumerate(OFFSETS):
        @pl.when(exists(o))
        def _():
            req_copy(i).wait_send()

        @pl.when(exists(-o))
        def _():
            far_copy(i).wait_send()
    for side, o in ((0, -1), (1, 1)):
        @pl.when(exists(o))
        def _():
            halo_copy(side).wait_send()
    for buf, sem in ((rs_out, rs_s), (ag, ag_s), (cn_out, cn_s), (cs_out, cs_s), (ag2, ag2_s)):
        wait_bytes(buf, sem)


def mix(step, tok_dev, place, start_ref, sp, gout, grow_ref, wo, out_ref):
    c = pl.program_id(0)
    at = c * step
    pairs = sp.shape[1]
    pos = start_ref[0] + at + lax.broadcasted_iota(jnp.int32, (step, NG), 0)
    one = jnp.where(pos == grow_ref[...], 1.0, 0.0)
    is_g = jnp.max(one, axis=-1, keepdims=True) > 0.5
    put = jnp.dot(one.astype(BF), gout[...], preferred_element_type=F32)
    own = jnp.concatenate(
        [
            jnp.concatenate([sp[place[c * (step // BLK) + i], p] for p in range(pairs)], axis=1)
            for i in range(step // BLK)
        ],
        axis=0,
    )
    att = jnp.where(is_g, put, own.astype(F32)).astype(BF)
    out_ref[...] = jnp.dot(att, wo[...], preferred_element_type=F32).astype(BF)


def body(n, tokens, w_query, w_key, w_value, w_out, rand_blocks, global_pos):
    tok_dev, width = tokens.shape
    nblk = tok_dev // BLK
    pairs = width // LANES
    cb = 256 if n <= 32 else 128
    rb = NG * width // (n * cb)
    ext = nblk + 2 + NFAR + NG // BLK
    dma = pltpu.SemaphoreType.DMA
    vm = pltpu.VMEM
    square = vm((width, width), BF)
    piece = vm((n, rb, cb), BF)
    stat = vm((n, rb, LANES), F32)
    keys = (3 + RAND) * BLK + NG
    big = vm((2, pairs // 2, 2 * BLK, keys), F32)
    small = vm((2, pairs // 2, 2 * BLK, LANES), F32)
    scratch = [
        vm((tok_dev, width), BF), square, square, square,
        vm((nblk, pairs, BLK, LANES), BF), vm((ext, 2, pairs, BLK, LANES), BF),
        vm((NG, width), BF), vm((pairs, NG, LANES), BF), vm((NG, width), F32),
        vm((NG, tok_dev), BF),
        vm((NFAR, 2, pairs, BLK, LANES), BF), vm((2 + NFAR, 2, pairs, BLK, LANES), BF),
        vm((NFAR, 8, LANES), jnp.int32), vm((NFAR, 8, LANES), jnp.int32),
        pltpu.SMEM((nblk,), jnp.int32),
        piece, piece, piece, piece, piece, stat, stat, piece,
        big, small, big, small,
        dma((4,)), dma((NFAR,)), dma((NFAR,)), dma((2 + NFAR,)), dma((2 + NFAR,)),
    ] + [dma(())] * 10
    anyspace = pl.BlockSpec(memory_space=pl.ANY)
    vmem = pl.BlockSpec(memory_space=pltpu.VMEM)
    smem = pl.BlockSpec(memory_space=pltpu.SMEM)
    grow = global_pos.reshape(1, NG)
    rbt = rand_blocks.T
    sp, gout, place = pl.pallas_call(
        functools.partial(attention, n),
        out_shape=(
            jax.ShapeDtypeStruct((nblk, pairs, BLK, LANES), BF),
            jax.ShapeDtypeStruct((NG, width), BF),
            jax.ShapeDtypeStruct((nblk,), jnp.int32),
        ),
        in_specs=[anyspace] * 4 + [vmem] * 2 + [smem],
        out_specs=(vmem, vmem, smem),
        scratch_shapes=scratch,
        compiler_params=pltpu.CompilerParams(
            collective_id=0, has_side_effects=True, vmem_limit_bytes=48 << 20
        ),
        name="attention",
    )(tokens, w_query, w_key, w_value, rbt, grow, rbt)
    step = 256
    start = (lax.axis_index("seq") * tok_dev).reshape(1).astype(jnp.int32)
    return pl.pallas_call(
        functools.partial(mix, step, tok_dev),
        grid=(tok_dev // step,),
        out_shape=jax.ShapeDtypeStruct((tok_dev, width), BF),
        in_specs=[smem, smem, vmem, vmem, vmem, vmem],
        out_specs=pl.BlockSpec((step, width), lambda i: (i, 0)),
        compiler_params=pltpu.CompilerParams(vmem_limit_bytes=32 << 20),
        name="mix",
    )(place, start, sp, gout, grow, w_out)


def solution(mesh):
    placed = (P("seq", None), P(), P(), P(), P(), P("seq", None), P())
    return jax.shard_map(
        functools.partial(body, mesh.shape["seq"]), mesh=mesh, in_specs=placed,
        out_specs=P("seq", None), check_vma=False,
    )
```

```python
import functools
import math

import jax
import jax.numpy as jnp
from jax import lax
from jax.experimental import pallas as pl
from jax.experimental.pallas import tpu as pltpu
from jax.sharding import PartitionSpec as P

HEADS = 16
HD = 64
BLK = 64
RAND = 3
NG = 128
FAR = 3
OFFSETS = tuple(range(-FAR, 0)) + tuple(range(1, FAR + 1))
NFAR = len(OFFSETS)
LANES = 128
EXP_SCALE = math.log2(math.e) / math.sqrt(HD)
SCORE_SCALE = 1.0 / math.sqrt(HD)
MESH = pl.DeviceIdType.MESH
BF = jnp.bfloat16
F32 = jnp.float32
NT = (((1,), (1,)), ((), ()))


def attention(
    n,
    tok_hbm, wq_hbm, wk_hbm, wv_hbm, rbv_ref, grow_ref, rb_ref,
    sp, gout, place,
    xt, wall, kv, xg, gf, sel, far, land,
    req_out, reqin, order,
    rs_out, rs_pair, rs_mid, rs_in, ag, cn_out, cn_pair, cn_mid, cn_in,
    cs_out, cs_pair, cs_mid, cs_in, ag2,
    sc, top, ex, inv,
    load_sem, req_s, req_r, edge_s, edge_r, one_s, one_r, all_s, all_r,
):
    nblk, _, width = tok_hbm.shape
    tok_dev = nblk * BLK
    me = lax.axis_index("seq")
    core, chip = lax.rem(me, 2), lax.div(me, 2)
    mate = me + 1 - 2 * core
    _, nc, rb, cb = ag.shape
    ncg = width // cb
    hpb = cb // HD
    pairs = width // LANES
    right0 = nblk + 1
    far0 = nblk + 2
    glob0 = far0 + NFAR
    gblk = NG // BLK

    loads = [
        pltpu.make_async_copy(src, dst, load_sem.at[i])
        for i, (src, dst) in enumerate(
            (
                (tok_hbm, xt), (wk_hbm, wall.at[0]), (wv_hbm, wall.at[1]),
                (wq_hbm, wall.at[2]),
            )
        )
    ]
    for cp in loads:
        cp.start()

    land[...] = jnp.zeros(land.shape, BF)
    reqin[...] = jnp.zeros(reqin.shape, jnp.int32)
    base = rbv_ref[RAND - 1:RAND, :] - me * nblk
    for i, o in enumerate(OFFSETS):
        loc = base - o * nblk
        loc = jnp.where((loc >= 0) & (loc < nblk), loc, 0)
        want = jnp.sum(loc, axis=1, keepdims=True)
        req_out[i] = jnp.broadcast_to(want, (8, LANES))

    barrier = pltpu.get_barrier_semaphore()

    def greet(o, c):
        pl.semaphore_signal(
            barrier, inc=1, device_id=(lax.rem(me + o, n),), device_id_type=MESH
        )
        return c

    lax.fori_loop(1, n, greet, 0)
    pl.semaphore_wait(barrier, n - 1)

    def to_chips(src, dst, i):
        def one(o, c):
            peer = lax.rem(chip + o, nc)
            pltpu.make_async_remote_copy(
                src_ref=src(peer), dst_ref=dst, send_sem=all_s.at[i], recv_sem=all_r.at[i],
                device_id=(2 * peer + core,), device_id_type=MESH,
            ).start()
            return c

        lax.fori_loop(1, nc, one, 0)

    def wait_chips(buf, sem):
        part = buf.at[pl.ds(0, nc - 1)]
        pltpu.make_async_copy(part, part, sem).wait()

    def to_mate(src, dst, i):
        return pltpu.make_async_remote_copy(
            src_ref=src, dst_ref=dst, send_sem=one_s.at[i], recv_sem=one_r.at[i],
            device_id=(mate,), device_id_type=MESH,
        )

    rs_mate = to_mate(rs_out.at[1 - core], rs_pair, 0)
    ag_mate = to_mate(ag.at[core], ag.at[core], 1)
    cs_mate = to_mate(cs_out.at[1 - core], cs_pair, 2)
    cn_mate = to_mate(cn_out.at[1 - core], cn_pair, 3)
    ag2_mate = to_mate(ag2.at[core], ag2.at[core], 4)

    def req_copy(i):
        return pltpu.make_async_remote_copy(
            src_ref=req_out.at[i], dst_ref=reqin.at[i], send_sem=req_s.at[i],
            recv_sem=req_r.at[i], device_id=(me + OFFSETS[i],), device_id_type=MESH,
        )

    def far_copy(i):
        return pltpu.make_async_remote_copy(
            src_ref=far.at[i],
            dst_ref=land.at[2 + i],
            send_sem=edge_s.at[2 + i], recv_sem=edge_r.at[2 + i],
            device_id=(me - OFFSETS[i],), device_id_type=MESH,
        )

    def halo_copy(side):
        src, dst, dev = (0, 1, me - 1) if side == 0 else (nblk - 1, 0, me + 1)
        return pltpu.make_async_remote_copy(
            src_ref=xt.at[src], dst_ref=land.at[dst],
            send_sem=edge_s.at[side], recv_sem=edge_r.at[side],
            device_id=(dev,), device_id_type=MESH,
        )

    def exists(o):
        return me + o >= 0 if o < 0 else me + o < n

    for i, o in enumerate(OFFSETS):
        @pl.when(exists(o))
        def _():
            req_copy(i).start()

    diag = lax.broadcasted_iota(jnp.int32, (NG, NG), 0) == lax.broadcasted_iota(
        jnp.int32, (NG, NG), 1
    )
    gcol = jnp.sum(
        jnp.where(diag, (grow_ref[...] - me * tok_dev).astype(F32), 0.0), axis=1, keepdims=True
    )
    hit = gcol == lax.broadcasted_iota(jnp.int32, (NG, tok_dev), 1).astype(F32)
    sel[...] = jnp.where(hit, 1.0, 0.0).astype(BF)

    loads[0].wait()
    picked = jnp.dot(sel[...], xt[...].reshape(tok_dev, width), preferred_element_type=F32)
    if rb % 16 == 0:
        picked = picked.astype(BF)
        for d in range(n):
            r, c = (d // ncg) * rb, (d % ncg) * cb
            rs_out[d % 2, d // 2] = picked[r:r + rb, c:c + cb]
    else:
        gf[...] = picked
        for d in range(n):
            r, c = (d // ncg) * rb, (d % ncg) * cb
            rs_out[d % 2, d // 2] = gf[r:r + rb, c:c + cb].astype(BF)
    rs_mate.start()

    def reduce_pair():
        rs_mate.wait_recv()
        rs_mid[...] = rs_out[core] + rs_pair[...]
        to_chips(lambda p: rs_mid.at[p], rs_in.at[chip], 0)
        rs_in[chip] = rs_mid[chip]

    def gather():
        wait_chips(rs_in, all_r.at[0])
        ag[core, chip] = jnp.sum(rs_in[...].astype(F32), axis=0).astype(BF)
        to_chips(lambda p: ag.at[core, chip], ag.at[core, chip], 1)

    def send_edges():
        for side, o in ((0, -1), (1, 1)):
            @pl.when(exists(o))
            def _():
                halo_copy(side).start()
        for i, o in enumerate(OFFSETS):
            @pl.when(exists(-o))
            def _():
                req_copy(i).wait_recv()
        for i, o in enumerate(OFFSETS):
            want = jnp.minimum(jnp.maximum(reqin[i, 0, 0], 0), nblk - 1)
            far[i] = xt[want]

            @pl.when(exists(-o))
            def _():
                far_copy(i).start()

    def gather_pair():
        wait_chips(ag.at[0], all_r.at[1])
        ag_mate.start()

    step = 512
    parts = tok_dev // step

    def project(c, carry):
        for i in range(3):
            @pl.when(c == i * parts)
            def _():
                loads[1 + i].wait()

        for at, act in ((1, reduce_pair), (3, gather), (3, send_edges), (5, gather_pair)):
            @pl.when(c == at)
            def _():
                act()

        which, part = lax.div(c, parts), lax.rem(c, parts)
        rows = xt[pl.ds(part * (step // BLK), step // BLK)].reshape(step, width)
        val = jnp.dot(rows, wall[which], preferred_element_type=F32).astype(BF)
        for p in range(pairs):
            kv[pl.ds(1 + part * (step // BLK), step // BLK), which, p] = val[
                :, p * LANES:(p + 1) * LANES
            ].reshape(step // BLK, BLK, LANES)
        return carry

    lax.fori_loop(0, 3 * parts, project, 0)

    lates = []
    for b in range(1, nblk - 1):
        r = rb_ref[RAND - 1, b] - me * nblk
        lates.append(jnp.where((r >= 0) & (r < nblk), 0, 1))
    early = nblk - 2 - sum(lates)
    seen = jnp.int32(0)
    spots = []
    for b in range(1, nblk - 1):
        late = lates[b - 1]
        spots.append(jnp.where(late == 1, early + seen, b - 1 - seen))
        seen = seen + late
        place[b] = spots[b - 1]
    for t in range(nblk - 2):
        order[t] = sum(jnp.where(spots[b - 1] == t, b, 0) for b in range(1, nblk - 1))
    place[0] = nblk - 2
    place[nblk - 1] = nblk - 1

    ag_mate.wait_recv()
    for d in range(n):
        r, c = (d // ncg) * rb, (d % ncg) * cb
        if rb % 16 == 0:
            xg[r:r + rb, c:c + cb] = ag[d % 2, d // 2]
        else:
            gf[r:r + rb, c:c + cb] = ag[d % 2, d // 2].astype(F32)
    if rb % 16:
        xg[...] = gf[...].astype(BF)

    def project_global(i, carry):
        val = jnp.dot(xg[...], wall[i], preferred_element_type=F32).astype(BF)
        for p in range(pairs):
            kv[glob0:glob0 + gblk, i, p] = val[:, p * LANES:(p + 1) * LANES].reshape(
                gblk, BLK, LANES
            )
        return carry

    lax.fori_loop(0, 3, project_global, 0)

    lane = lax.broadcasted_iota(jnp.int32, (1, LANES), 1)
    islo = lane < HD
    halves = (jnp.where(islo, 1.0, 0.0).astype(BF), jnp.where(islo, 0.0, 1.0).astype(BF))
    wide_row = LANES // rb
    lane_f = jnp.bitwise_and(lane, wide_row - 1)
    own_row = lax.shift_right_logical(
        lax.broadcasted_iota(jnp.int32, (rb, LANES), 1), wide_row.bit_length() - 1
    ) == lax.broadcasted_iota(jnp.int32, (rb, LANES), 0)
    head_of = jnp.where(
        jnp.bitwise_and(lax.broadcasted_iota(jnp.int32, (LANES, cb), 0), wide_row - 1)
        == lax.shift_right_logical(lax.broadcasted_iota(jnp.int32, (LANES, cb), 1), 6),
        1.0, 0.0,
    )

    def flat(x):
        return jnp.sum(jnp.where(own_row, x, 0.0), axis=0, keepdims=True)

    def spread(x):
        rows = [jnp.where(own_row, x[i:i + 1], 0.0) for i in range(nc)]
        return jnp.dot(
            jnp.concatenate(rows, axis=0), head_of, preferred_element_type=F32,
            precision=lax.Precision.HIGHEST,
        )

    def stacked(x):
        return jnp.concatenate([x * m for m in halves], axis=0)

    def with_ones(x):
        return jnp.concatenate([x, jnp.ones(x.shape, BF)], axis=1)

    per = cb // LANES

    def global_part(cg, carry):
        nums, stat = [], jnp.zeros((NG, LANES), F32)
        for j in range(per):
            p = cg * per + j
            s = lax.dot_general(
                stacked(kv[glob0:glob0 + gblk, 2, p].reshape(NG, LANES)), kv[1:1 + nblk, 0, p].reshape(tok_dev, LANES), NT,
                preferred_element_type=F32,
            )
            m = jnp.max(s, axis=-1, keepdims=True)
            e = jnp.exp2((s - m) * EXP_SCALE).astype(BF)
            x = jnp.dot(
                e, with_ones(kv[1:1 + nblk, 1, p].reshape(tok_dev, LANES)),
                preferred_element_type=F32,
            )
            nums.append(jnp.where(islo, x[:NG, :LANES], x[NG:, :LANES]).astype(BF))
            m = m * SCORE_SCALE
            for h in range(2):
                rows = slice(h * NG, (h + 1) * NG)
                stat = jnp.where(lane_f == 2 * j + h, m[rows], stat)
                stat = jnp.where(lane_f == hpb + 2 * j + h, x[rows, LANES:], stat)
        num = jnp.concatenate(nums, axis=1) if per > 1 else nums[0]
        for rg in range(NG // rb):
            d = rg * ncg + cg
            k, c = lax.rem(d, 2), lax.div(d, 2)
            cn_out[k, c] = num[rg * rb:(rg + 1) * rb]
            cs_out[k, c] = flat(stat[rg * rb:(rg + 1) * rb])
        return carry

    lax.fori_loop(0, ncg, global_part, 0)
    cs_mate.start()
    cn_mate.start()

    def merge_pair():
        cs_mate.wait_recv()
        cn_mate.wait_recv()
        a, b = cs_out[core].reshape(nc, LANES), cs_pair[...].reshape(nc, LANES)
        m = jnp.maximum(a, b)
        ea, eb = jnp.exp(a - m), jnp.exp(b - m)
        t = a * pltpu.roll(ea, hpb, 1) + b * pltpu.roll(eb, hpb, 1)
        cs_mid[...] = jnp.where(lane_f < hpb, m, t).reshape(nc, 1, LANES)
        clean = lane_f < hpb
        fa, fb = spread(jnp.where(clean, ea, 0.0)), spread(jnp.where(clean, eb, 0.0))
        for i in range(nc):
            rows = slice(i * rb, (i + 1) * rb)
            cn_mid[i] = (
                cn_out[core, i].astype(F32) * fa[rows] + cn_pair[i].astype(F32) * fb[rows]
            ).astype(BF)
        to_chips(lambda p: cs_mid.at[p], cs_in.at[chip], 2)
        to_chips(lambda p: cn_mid.at[p], cn_in.at[chip], 3)
        cs_in[chip] = cs_mid[chip]
        cn_in[chip] = cn_mid[chip]

    def choose(b):
        picks = []
        for r in range(RAND):
            rel = rb_ref[r, b] - me * nblk
            dev = lax.div(rel + FAR * nblk, nblk)
            slot = jnp.where(dev < FAR, dev, dev - 1)
            pick = jnp.where(dev == FAR, rel + 1, far0 + slot)
            picks.append(jnp.minimum(jnp.maximum(pick, 0), far0 + NFAR - 1))
        return picks

    def rows_of(which, p, b, picks):
        return jnp.concatenate(
            [kv[b + i, which, p] for i in range(3)]
            + [kv[i, which, p] for i in picks]
            + [kv[glob0 + i, which, p] for i in range(gblk)],
            axis=0,
        )

    half = pairs // 2
    nsub = (3 + RAND) * BLK // LANES + NG // LANES

    def wide(x):
        return jnp.concatenate([x] * nsub, axis=1)

    def scores(g, blk):
        t, b, picks, bias = blk
        for j in range(half):
            p = g * half + j
            s = lax.dot_general(
                stacked(kv[1 + b, 2, p]), rows_of(0, p, b, picks), NT, preferred_element_type=F32
            )
            if bias is not None:
                s = s + bias
            sc[g, j] = s
            top[g, j] = jnp.broadcast_to(
                jnp.max(s, axis=-1, keepdims=True), (2 * BLK, LANES)
            )

    def expo(g):
        for j in range(half):
            e = jnp.exp2((sc[g, j] - wide(top[g, j])) * EXP_SCALE)
            ex[g, j] = e
            inv[g, j] = jnp.broadcast_to(
                1.0 / jnp.sum(e, axis=-1, keepdims=True), (2 * BLK, LANES)
            )

    def weigh(g, blk):
        t, b, picks, _ = blk
        for j in range(0, half, 2):
            p = g * half + j
            w = jnp.concatenate(
                [(ex[g, j + i] * wide(inv[g, j + i])).astype(BF) for i in range(2)], axis=0
            )
            x = jnp.dot(
                w,
                jnp.concatenate([rows_of(1, p + i, b, picks) for i in range(2)], axis=1),
                preferred_element_type=F32,
            )
            for i in range(2):
                y = x[i * 2 * BLK:(i + 1) * 2 * BLK, i * LANES:(i + 1) * LANES]
                sp[t, p + i] = jnp.where(islo, y[:BLK], y[BLK:]).astype(BF)

    def attend(before, blocks):
        seq = [before] + blocks
        for i, blk in enumerate(blocks):
            expo(1)
            scores(0, blk)
            weigh(0, seq[i])
            expo(0)
            scores(1, blk)
            weigh(1, seq[i])

    def block_at(t, b, bias=None):
        return t, b, choose(b), bias

    def between():
        wait_chips(cs_in, all_r.at[2])
        wait_chips(cn_in, all_r.at[3])
        stat = cs_in[...].reshape(nc, LANES)
        e = jnp.exp(stat - jnp.max(stat, axis=0, keepdims=True))
        den = jnp.sum(pltpu.roll(stat, LANES - hpb, 1) * e, axis=0, keepdims=True)
        fac = spread(jnp.where(lane_f < hpb, e / den, 0.0))
        num = cn_in[0].astype(F32) * fac[0:rb]
        for i in range(1, nc):
            num = num + cn_in[i].astype(F32) * fac[i * rb:(i + 1) * rb]
        ag2[core, chip] = num.astype(BF)
        to_chips(lambda p: ag2.at[core, chip], ag2.at[core, chip], 4)

        for side, o in ((0, 1), (1, -1)):
            @pl.when(exists(o))
            def _():
                halo_copy(side).wait_recv()
        for i, o in enumerate(OFFSETS):
            @pl.when(exists(o))
            def _():
                far_copy(i).wait_recv()
        def project_edges(i, carry):
            rows = land[...].reshape((2 + NFAR) * BLK, width)
            val = jnp.dot(rows, wall[i], preferred_element_type=F32).astype(BF)
            for p in range(pairs):
                x = val[:, p * LANES:(p + 1) * LANES].reshape(2 + NFAR, BLK, LANES)
                kv[0, i, p] = x[0]
                kv[right0:glob0, i, p] = x[1:]
            return carry

        lax.fori_loop(0, 2, project_edges, 0)

    def two(i, carry):
        @pl.when(i == 1)
        def _():
            merge_pair()

        @pl.when(i == nblk // 4)
        def _():
            between()

        @pl.when(i == nblk // 4 + 2)
        def _():
            wait_chips(ag2.at[0], all_r.at[4])
            ag2_mate.start()

        prev = jnp.maximum(2 * i - 1, 0)
        attend(
            block_at(prev, order[prev]),
            [block_at(2 * i + j, order[2 * i + j]) for j in range(2)],
        )
        return carry

    lax.fori_loop(0, nblk // 2 - 1, two, 0)
    key_col = lax.broadcasted_iota(jnp.int32, (1, (3 + RAND) * BLK + NG), 1)
    lead = jnp.where(me == 0, BLK, 0)
    tail = jnp.where(me == n - 1, 2 * BLK, 3 * BLK)
    first = jnp.where(key_col < lead, -1e30, 0.0)
    last = jnp.where((key_col >= tail) & (key_col < 3 * BLK), -1e30, 0.0)
    end = block_at(nblk - 1, nblk - 1, last)
    attend(block_at(nblk - 3, order[nblk - 3]), [block_at(nblk - 2, 0, first), end])
    expo(1)
    weigh(0, end)
    weigh(1, end)

    ag2_mate.wait_recv()
    for d in range(n):
        r, c = (d // ncg) * rb, (d % ncg) * cb
        if rb % 16 == 0:
            gout[r:r + rb, c:c + cb] = ag2[d % 2, d // 2]
        else:
            gf[r:r + rb, c:c + cb] = ag2[d % 2, d // 2].astype(F32)
    if rb % 16:
        gout[...] = gf[...].astype(BF)

    for i, o in enumerate(OFFSETS):
        @pl.when(exists(o))
        def _():
            req_copy(i).wait_send()

        @pl.when(exists(-o))
        def _():
            far_copy(i).wait_send()
    for side, o in ((0, -1), (1, 1)):
        @pl.when(exists(o))
        def _():
            halo_copy(side).wait_send()
    for cp in (rs_mate, ag_mate, cs_mate, cn_mate, ag2_mate):
        cp.wait_send()
    for i, buf in enumerate((rs_mid, ag.at[0], cs_mid, cn_mid, ag2.at[0])):
        wait_chips(buf, all_s.at[i])


def mix(step, tok_dev, place, start_ref, sp, gout, grow_ref, wo, out_ref):
    c = pl.program_id(0)
    at = c * step
    pairs = sp.shape[1]
    pos = start_ref[0] + at + lax.broadcasted_iota(jnp.int32, (step, NG), 0)
    one = jnp.where(pos == grow_ref[...], 1.0, 0.0)
    is_g = jnp.max(one, axis=-1, keepdims=True) > 0.5
    put = jnp.dot(one.astype(BF), gout[...], preferred_element_type=F32)
    own = jnp.concatenate(
        [
            jnp.concatenate([sp[place[c * (step // BLK) + i], p] for p in range(pairs)], axis=1)
            for i in range(step // BLK)
        ],
        axis=0,
    )
    att = jnp.where(is_g, put, own.astype(F32)).astype(BF)
    out_ref[...] = jnp.dot(att, wo[...], preferred_element_type=F32).astype(BF)


def body(n, tokens, w_query, w_key, w_value, w_out, rand_blocks, global_pos):
    tok_dev, width = tokens.shape
    nblk = tok_dev // BLK
    pairs = width // LANES
    cb = 256 if n <= 32 else 128
    rb = NG * width // (n * cb)
    ext = nblk + 2 + NFAR + NG // BLK
    dma = pltpu.SemaphoreType.DMA
    vm = pltpu.VMEM
    nc = n // 2
    both = vm((2, nc, rb, cb), BF)
    piece = vm((nc, rb, cb), BF)
    stat = vm((nc, 1, LANES), F32)
    keys = (3 + RAND) * BLK + NG
    big = vm((2, pairs // 2, 2 * BLK, keys), F32)
    small = vm((2, pairs // 2, 2 * BLK, LANES), F32)
    scratch = [
        vm((nblk, BLK, width), BF), vm((3, width, width), BF),
        vm((ext, 3, pairs, BLK, LANES), BF),
        vm((NG, width), BF), vm((NG, width), F32), vm((NG, tok_dev), BF),
        vm((NFAR, BLK, width), BF), vm((2 + NFAR, BLK, width), BF),
        vm((NFAR, 8, LANES), jnp.int32), vm((NFAR, 8, LANES), jnp.int32),
        pltpu.SMEM((nblk,), jnp.int32),
        both, piece, piece, piece, both, both, piece, piece, piece,
        vm((2, nc, 1, LANES), F32), stat, stat, stat, both,
        big, small, big, small,
        dma((4,)), dma((NFAR,)), dma((NFAR,)), dma((2 + NFAR,)), dma((2 + NFAR,)),
        dma((5,)), dma((5,)), dma((5,)), dma((5,)),
    ]
    anyspace = pl.BlockSpec(memory_space=pl.ANY)
    vmem = pl.BlockSpec(memory_space=pltpu.VMEM)
    smem = pl.BlockSpec(memory_space=pltpu.SMEM)
    grow = global_pos.reshape(1, NG)
    rbt = rand_blocks.T
    sp, gout, place = pl.pallas_call(
        functools.partial(attention, n),
        out_shape=(
            jax.ShapeDtypeStruct((nblk, pairs, BLK, LANES), BF),
            jax.ShapeDtypeStruct((NG, width), BF),
            jax.ShapeDtypeStruct((nblk,), jnp.int32),
        ),
        in_specs=[anyspace] * 4 + [vmem] * 2 + [smem],
        out_specs=(vmem, vmem, smem),
        scratch_shapes=scratch,
        compiler_params=pltpu.CompilerParams(
            collective_id=0, has_side_effects=True, vmem_limit_bytes=59 << 20
        ),
        name="attention",
    )(tokens.reshape(nblk, BLK, width), w_query, w_key, w_value, rbt, grow, rbt)
    step = 256
    start = (lax.axis_index("seq") * tok_dev).reshape(1).astype(jnp.int32)
    return pl.pallas_call(
        functools.partial(mix, step, tok_dev),
        grid=(tok_dev // step,),
        out_shape=jax.ShapeDtypeStruct((tok_dev, width), BF),
        in_specs=[smem, smem, vmem, vmem, vmem, vmem],
        out_specs=pl.BlockSpec((step, width), lambda i: (i, 0)),
        compiler_params=pltpu.CompilerParams(vmem_limit_bytes=32 << 20),
        name="mix",
    )(place, start, sp, gout, grow, w_out)


def solution(mesh):
    placed = (P("seq", None), P(), P(), P(), P(), P("seq", None), P())
    return jax.shard_map(
        functools.partial(body, mesh.shape["seq"]), mesh=mesh, in_specs=placed,
        out_specs=P("seq", None), check_vma=False,
    )
```

```python
import functools
import math

import jax
import jax.numpy as jnp
from jax import lax
from jax.experimental import pallas as pl
from jax.experimental.pallas import tpu as pltpu
from jax.sharding import PartitionSpec as P

HEADS = 16
HD = 64
BLK = 64
RAND = 3
NG = 128
FAR = 3
OFFSETS = tuple(range(-FAR, 0)) + tuple(range(1, FAR + 1))
NFAR = len(OFFSETS)
LANES = 128
EXP_SCALE = math.log2(math.e) / math.sqrt(HD)
SCORE_SCALE = 1.0 / math.sqrt(HD)
MESH = pl.DeviceIdType.MESH
BF = jnp.bfloat16
F32 = jnp.float32
NT = (((1,), (1,)), ((), ()))


def attention(
    n,
    tok_hbm, wq_hbm, wk_hbm, wv_hbm, rbv_ref, grow_ref, rb_ref,
    sp, gout, place,
    xt, wall, kv, xg, gf, sel, far, land,
    req_out, reqin, order,
    rs_out, rs_pair, rs_mid, rs_in, ag, cn_out, cn_pair, cn_mid, cn_in,
    cs_out, cs_pair, cs_mid, cs_in, ag2,
    sc, top, ex, inv,
    load_sem, req_s, req_r, edge_s, edge_r, one_s, one_r, all_s, all_r,
):
    nblk, _, width = tok_hbm.shape
    tok_dev = nblk * BLK
    me = lax.axis_index("seq")
    core, chip = lax.rem(me, 2), lax.div(me, 2)
    mate = me + 1 - 2 * core
    _, nc, rb, cb = ag.shape
    ncg = width // cb
    hpb = cb // HD
    pairs = width // LANES
    right0 = nblk + 1
    far0 = nblk + 2
    glob0 = far0 + NFAR
    gblk = NG // BLK

    loads = [
        pltpu.make_async_copy(src, dst, load_sem.at[i])
        for i, (src, dst) in enumerate(
            (
                (tok_hbm, xt), (wk_hbm, wall.at[0]), (wv_hbm, wall.at[1]),
                (wq_hbm, wall.at[2]),
            )
        )
    ]
    for cp in loads:
        cp.start()

    land[...] = jnp.zeros(land.shape, BF)
    reqin[...] = jnp.zeros(reqin.shape, jnp.int32)
    base = rbv_ref[RAND - 1:RAND, :] - me * nblk
    for i, o in enumerate(OFFSETS):
        loc = base - o * nblk
        loc = jnp.where((loc >= 0) & (loc < nblk), loc, 0)
        want = jnp.sum(loc, axis=1, keepdims=True)
        req_out[i] = jnp.broadcast_to(want, (8, LANES))

    def exists(o):
        return me + o >= 0 if o < 0 else me + o < n

    barrier = pltpu.get_barrier_semaphore()
    other = me - 1 + 2 * core

    def greet(device):
        pl.semaphore_signal(barrier, inc=1, device_id=(device,), device_id_type=MESH)

    def greet_chip(o, c):
        greet(2 * lax.rem(chip + o, nc) + core)
        return c

    lax.fori_loop(1, nc, greet_chip, 0)
    greet(mate)
    there = ((other >= 0) & (other < n), other), (exists(-FAR), me - FAR), (exists(FAR), me + FAR)
    for ok, device in there:
        @pl.when(ok)
        def _():
            greet(device)

    def to_chips(src, dst, i):
        def one(o, c):
            peer = lax.rem(chip + o, nc)
            pltpu.make_async_remote_copy(
                src_ref=src(peer), dst_ref=dst, send_sem=all_s.at[i], recv_sem=all_r.at[i],
                device_id=(2 * peer + core,), device_id_type=MESH,
            ).start()
            return c

        lax.fori_loop(1, nc, one, 0)

    def wait_chips(buf, sem):
        part = buf.at[pl.ds(0, nc - 1)]
        pltpu.make_async_copy(part, part, sem).wait()

    def to_mate(src, dst, i):
        return pltpu.make_async_remote_copy(
            src_ref=src, dst_ref=dst, send_sem=one_s.at[i], recv_sem=one_r.at[i],
            device_id=(mate,), device_id_type=MESH,
        )

    rs_mate = to_mate(rs_out.at[1 - core], rs_pair, 0)
    ag_mate = to_mate(ag.at[core], ag.at[core], 1)
    cs_mate = to_mate(cs_out.at[1 - core], cs_pair, 2)
    cn_mate = to_mate(cn_out.at[1 - core], cn_pair, 3)
    ag2_mate = to_mate(ag2.at[core], ag2.at[core], 4)

    def req_copy(i):
        return pltpu.make_async_remote_copy(
            src_ref=req_out.at[i], dst_ref=reqin.at[i], send_sem=req_s.at[i],
            recv_sem=req_r.at[i], device_id=(me + OFFSETS[i],), device_id_type=MESH,
        )

    def far_copy(i):
        return pltpu.make_async_remote_copy(
            src_ref=far.at[i],
            dst_ref=land.at[2 + i],
            send_sem=edge_s.at[2 + i], recv_sem=edge_r.at[2 + i],
            device_id=(me - OFFSETS[i],), device_id_type=MESH,
        )

    def halo_copy(side):
        src, dst, dev = (0, 1, me - 1) if side == 0 else (nblk - 1, 0, me + 1)
        return pltpu.make_async_remote_copy(
            src_ref=xt.at[src], dst_ref=land.at[dst],
            send_sem=edge_s.at[side], recv_sem=edge_r.at[side],
            device_id=(dev,), device_id_type=MESH,
        )

    diag = lax.broadcasted_iota(jnp.int32, (NG, NG), 0) == lax.broadcasted_iota(
        jnp.int32, (NG, NG), 1
    )
    gcol = jnp.sum(
        jnp.where(diag, (grow_ref[...] - me * tok_dev).astype(F32), 0.0), axis=1, keepdims=True
    )
    hit = gcol == lax.broadcasted_iota(jnp.int32, (NG, tok_dev), 1).astype(F32)
    sel[...] = jnp.where(hit, 1.0, 0.0).astype(BF)

    loads[0].wait()
    picked = jnp.dot(sel[...], xt[...].reshape(tok_dev, width), preferred_element_type=F32)
    if rb % 16 == 0:
        picked = picked.astype(BF)
        for d in range(n):
            r, c = (d // ncg) * rb, (d % ncg) * cb
            rs_out[d % 2, d // 2] = picked[r:r + rb, c:c + cb]
    else:
        gf[...] = picked
        for d in range(n):
            r, c = (d // ncg) * rb, (d % ncg) * cb
            rs_out[d % 2, d // 2] = gf[r:r + rb, c:c + cb].astype(BF)
    pl.semaphore_wait(barrier, nc + sum(jnp.where(ok, 1, 0) for ok, _ in there))
    rs_mate.start()
    for i, o in enumerate(OFFSETS):
        @pl.when(exists(o))
        def _():
            req_copy(i).start()


    def reduce_pair():
        rs_mate.wait_recv()
        rs_mid[...] = rs_out[core] + rs_pair[...]
        to_chips(lambda p: rs_mid.at[p], rs_in.at[chip], 0)
        rs_in[chip] = rs_mid[chip]

    def gather():
        wait_chips(rs_in, all_r.at[0])
        ag[core, chip] = jnp.sum(rs_in[...].astype(F32), axis=0).astype(BF)
        to_chips(lambda p: ag.at[core, chip], ag.at[core, chip], 1)

    def send_edges():
        for side, o in ((0, -1), (1, 1)):
            @pl.when(exists(o))
            def _():
                halo_copy(side).start()
        for i, o in enumerate(OFFSETS):
            @pl.when(exists(-o))
            def _():
                req_copy(i).wait_recv()
        for i, o in enumerate(OFFSETS):
            want = jnp.minimum(jnp.maximum(reqin[i, 0, 0], 0), nblk - 1)
            far[i] = xt[want]

            @pl.when(exists(-o))
            def _():
                far_copy(i).start()

    def gather_pair():
        wait_chips(ag.at[0], all_r.at[1])
        ag_mate.start()

    step = 512
    parts = tok_dev // step

    def project(c, carry):
        for i in range(3):
            @pl.when(c == i * parts)
            def _():
                loads[1 + i].wait()

        for at, act in ((1, reduce_pair), (3, gather), (3, send_edges), (5, gather_pair)):
            @pl.when(c == at)
            def _():
                act()

        which, part = lax.div(c, parts), lax.rem(c, parts)
        rows = xt[pl.ds(part * (step // BLK), step // BLK)].reshape(step, width)
        val = jnp.dot(rows, wall[which], preferred_element_type=F32).astype(BF)
        for p in range(pairs):
            kv[pl.ds(1 + part * (step // BLK), step // BLK), which, p] = val[
                :, p * LANES:(p + 1) * LANES
            ].reshape(step // BLK, BLK, LANES)
        return carry

    lax.fori_loop(0, 3 * parts, project, 0)

    lates = []
    for b in range(1, nblk - 1):
        r = rb_ref[RAND - 1, b] - me * nblk
        lates.append(jnp.where((r >= 0) & (r < nblk), 0, 1))
    early = nblk - 2 - sum(lates)
    seen = jnp.int32(0)
    spots = []
    for b in range(1, nblk - 1):
        late = lates[b - 1]
        spots.append(jnp.where(late == 1, early + seen, b - 1 - seen))
        seen = seen + late
        place[b] = spots[b - 1]
    for t in range(nblk - 2):
        order[t] = sum(jnp.where(spots[b - 1] == t, b, 0) for b in range(1, nblk - 1))
    place[0] = nblk - 2
    place[nblk - 1] = nblk - 1

    ag_mate.wait_recv()
    for d in range(n):
        r, c = (d // ncg) * rb, (d % ncg) * cb
        if rb % 16 == 0:
            xg[r:r + rb, c:c + cb] = ag[d % 2, d // 2]
        else:
            gf[r:r + rb, c:c + cb] = ag[d % 2, d // 2].astype(F32)
    if rb % 16:
        xg[...] = gf[...].astype(BF)

    def project_global(i, carry):
        val = jnp.dot(xg[...], wall[i], preferred_element_type=F32).astype(BF)
        for p in range(pairs):
            kv[glob0:glob0 + gblk, i, p] = val[:, p * LANES:(p + 1) * LANES].reshape(
                gblk, BLK, LANES
            )
        return carry

    lax.fori_loop(0, 3, project_global, 0)

    lane = lax.broadcasted_iota(jnp.int32, (1, LANES), 1)
    islo = lane < HD
    halves = (jnp.where(islo, 1.0, 0.0).astype(BF), jnp.where(islo, 0.0, 1.0).astype(BF))
    wide_row = LANES // rb
    lane_f = jnp.bitwise_and(lane, wide_row - 1)
    own_row = lax.shift_right_logical(
        lax.broadcasted_iota(jnp.int32, (rb, LANES), 1), wide_row.bit_length() - 1
    ) == lax.broadcasted_iota(jnp.int32, (rb, LANES), 0)
    head_of = jnp.where(
        jnp.bitwise_and(lax.broadcasted_iota(jnp.int32, (LANES, cb), 0), wide_row - 1)
        == lax.shift_right_logical(lax.broadcasted_iota(jnp.int32, (LANES, cb), 1), 6),
        1.0, 0.0,
    )

    def flat(x):
        return jnp.sum(jnp.where(own_row, x, 0.0), axis=0, keepdims=True)

    def spread(x):
        rows = [jnp.where(own_row, x[i:i + 1], 0.0) for i in range(nc)]
        return jnp.dot(
            jnp.concatenate(rows, axis=0), head_of, preferred_element_type=F32,
            precision=lax.Precision.HIGHEST,
        )

    def stacked(x):
        return jnp.concatenate([x * m for m in halves], axis=0)

    def with_ones(x):
        return jnp.concatenate([x, jnp.ones(x.shape, BF)], axis=1)

    per = cb // LANES

    def global_part(cg, carry):
        nums, stat = [], jnp.zeros((NG, LANES), F32)
        for j in range(per):
            p = cg * per + j
            s = lax.dot_general(
                stacked(kv[glob0:glob0 + gblk, 2, p].reshape(NG, LANES)), kv[1:1 + nblk, 0, p].reshape(tok_dev, LANES), NT,
                preferred_element_type=F32,
            )
            m = jnp.max(s, axis=-1, keepdims=True)
            e = jnp.exp2((s - m) * EXP_SCALE).astype(BF)
            x = jnp.dot(
                e, with_ones(kv[1:1 + nblk, 1, p].reshape(tok_dev, LANES)),
                preferred_element_type=F32,
            )
            nums.append(jnp.where(islo, x[:NG, :LANES], x[NG:, :LANES]).astype(BF))
            m = m * SCORE_SCALE
            for h in range(2):
                rows = slice(h * NG, (h + 1) * NG)
                stat = jnp.where(lane_f == 2 * j + h, m[rows], stat)
                stat = jnp.where(lane_f == hpb + 2 * j + h, x[rows, LANES:], stat)
        num = jnp.concatenate(nums, axis=1) if per > 1 else nums[0]
        for rg in range(NG // rb):
            d = rg * ncg + cg
            k, c = lax.rem(d, 2), lax.div(d, 2)
            cn_out[k, c] = num[rg * rb:(rg + 1) * rb]
            cs_out[k, c] = flat(stat[rg * rb:(rg + 1) * rb])
        return carry

    lax.fori_loop(0, ncg, global_part, 0)
    cs_mate.start()
    cn_mate.start()

    def merge_pair():
        cs_mate.wait_recv()
        cn_mate.wait_recv()
        a, b = cs_out[core].reshape(nc, LANES), cs_pair[...].reshape(nc, LANES)
        m = jnp.maximum(a, b)
        ea, eb = jnp.exp(a - m), jnp.exp(b - m)
        t = a * pltpu.roll(ea, hpb, 1) + b * pltpu.roll(eb, hpb, 1)
        cs_mid[...] = jnp.where(lane_f < hpb, m, t).reshape(nc, 1, LANES)
        clean = lane_f < hpb
        fa, fb = spread(jnp.where(clean, ea, 0.0)), spread(jnp.where(clean, eb, 0.0))
        for i in range(nc):
            rows = slice(i * rb, (i + 1) * rb)
            cn_mid[i] = (
                cn_out[core, i].astype(F32) * fa[rows] + cn_pair[i].astype(F32) * fb[rows]
            ).astype(BF)
        to_chips(lambda p: cs_mid.at[p], cs_in.at[chip], 2)
        to_chips(lambda p: cn_mid.at[p], cn_in.at[chip], 3)
        cs_in[chip] = cs_mid[chip]
        cn_in[chip] = cn_mid[chip]

    def choose(b):
        picks = []
        for r in range(RAND):
            rel = rb_ref[r, b] - me * nblk
            dev = lax.div(rel + FAR * nblk, nblk)
            slot = jnp.where(dev < FAR, dev, dev - 1)
            pick = jnp.where(dev == FAR, rel + 1, far0 + slot)
            picks.append(jnp.minimum(jnp.maximum(pick, 0), far0 + NFAR - 1))
        return picks

    def rows_of(which, p, b, picks):
        return jnp.concatenate(
            [kv[b + i, which, p] for i in range(3)]
            + [kv[i, which, p] for i in picks]
            + [kv[glob0 + i, which, p] for i in range(gblk)],
            axis=0,
        )

    half = pairs // 2
    nsub = (3 + RAND) * BLK // LANES + NG // LANES

    def wide(x):
        return jnp.concatenate([x] * nsub, axis=1)

    def scores(g, blk):
        t, b, picks, bias = blk
        for j in range(half):
            p = g * half + j
            s = lax.dot_general(
                stacked(kv[1 + b, 2, p]), rows_of(0, p, b, picks), NT, preferred_element_type=F32
            )
            if bias is not None:
                s = s + bias
            sc[g, j] = s
            top[g, j] = jnp.broadcast_to(
                jnp.max(s, axis=-1, keepdims=True), (2 * BLK, LANES)
            )

    def expo(g):
        for j in range(half):
            e = jnp.exp2((sc[g, j] - wide(top[g, j])) * EXP_SCALE)
            ex[g, j] = e
            inv[g, j] = jnp.broadcast_to(
                1.0 / jnp.sum(e, axis=-1, keepdims=True), (2 * BLK, LANES)
            )

    def weigh(g, blk):
        t, b, picks, _ = blk
        for j in range(0, half, 2):
            p = g * half + j
            w = jnp.concatenate(
                [(ex[g, j + i] * wide(inv[g, j + i])).astype(BF) for i in range(2)], axis=0
            )
            x = jnp.dot(
                w,
                jnp.concatenate([rows_of(1, p + i, b, picks) for i in range(2)], axis=1),
                preferred_element_type=F32,
            )
            for i in range(2):
                y = x[i * 2 * BLK:(i + 1) * 2 * BLK, i * LANES:(i + 1) * LANES]
                sp[t, p + i] = jnp.where(islo, y[:BLK], y[BLK:]).astype(BF)

    def attend(before, blocks):
        seq = [before] + blocks
        for i, blk in enumerate(blocks):
            expo(1)
            scores(0, blk)
            weigh(0, seq[i])
            expo(0)
            scores(1, blk)
            weigh(1, seq[i])

    def block_at(t, b, bias=None):
        return t, b, choose(b), bias

    def between():
        wait_chips(cs_in, all_r.at[2])
        wait_chips(cn_in, all_r.at[3])
        stat = cs_in[...].reshape(nc, LANES)
        e = jnp.exp(stat - jnp.max(stat, axis=0, keepdims=True))
        den = jnp.sum(pltpu.roll(stat, LANES - hpb, 1) * e, axis=0, keepdims=True)
        fac = spread(jnp.where(lane_f < hpb, e / den, 0.0))
        num = cn_in[0].astype(F32) * fac[0:rb]
        for i in range(1, nc):
            num = num + cn_in[i].astype(F32) * fac[i * rb:(i + 1) * rb]
        ag2[core, chip] = num.astype(BF)
        to_chips(lambda p: ag2.at[core, chip], ag2.at[core, chip], 4)

        for side, o in ((0, 1), (1, -1)):
            @pl.when(exists(o))
            def _():
                halo_copy(side).wait_recv()
        for i, o in enumerate(OFFSETS):
            @pl.when(exists(o))
            def _():
                far_copy(i).wait_recv()
        def project_edges(i, carry):
            rows = land[...].reshape((2 + NFAR) * BLK, width)
            val = jnp.dot(rows, wall[i], preferred_element_type=F32).astype(BF)
            for p in range(pairs):
                x = val[:, p * LANES:(p + 1) * LANES].reshape(2 + NFAR, BLK, LANES)
                kv[0, i, p] = x[0]
                kv[right0:glob0, i, p] = x[1:]
            return carry

        lax.fori_loop(0, 2, project_edges, 0)

    def two(i, carry):
        @pl.when(i == 1)
        def _():
            merge_pair()

        @pl.when(i == nblk // 4)
        def _():
            between()

        @pl.when(i == nblk // 4 + 2)
        def _():
            wait_chips(ag2.at[0], all_r.at[4])
            ag2_mate.start()

        prev = jnp.maximum(2 * i - 1, 0)
        attend(
            block_at(prev, order[prev]),
            [block_at(2 * i + j, order[2 * i + j]) for j in range(2)],
        )
        return carry

    lax.fori_loop(0, nblk // 2 - 1, two, 0)
    key_col = lax.broadcasted_iota(jnp.int32, (1, (3 + RAND) * BLK + NG), 1)
    lead = jnp.where(me == 0, BLK, 0)
    tail = jnp.where(me == n - 1, 2 * BLK, 3 * BLK)
    first = jnp.where(key_col < lead, -1e30, 0.0)
    last = jnp.where((key_col >= tail) & (key_col < 3 * BLK), -1e30, 0.0)
    end = block_at(nblk - 1, nblk - 1, last)
    attend(block_at(nblk - 3, order[nblk - 3]), [block_at(nblk - 2, 0, first), end])
    expo(1)
    weigh(0, end)
    weigh(1, end)

    ag2_mate.wait_recv()
    for d in range(n):
        r, c = (d // ncg) * rb, (d % ncg) * cb
        if rb % 16 == 0:
            gout[r:r + rb, c:c + cb] = ag2[d % 2, d // 2]
        else:
            gf[r:r + rb, c:c + cb] = ag2[d % 2, d // 2].astype(F32)
    if rb % 16:
        gout[...] = gf[...].astype(BF)

    for i, o in enumerate(OFFSETS):
        @pl.when(exists(o))
        def _():
            req_copy(i).wait_send()

        @pl.when(exists(-o))
        def _():
            far_copy(i).wait_send()
    for side, o in ((0, -1), (1, 1)):
        @pl.when(exists(o))
        def _():
            halo_copy(side).wait_send()
    for cp in (rs_mate, ag_mate, cs_mate, cn_mate, ag2_mate):
        cp.wait_send()
    for i, buf in enumerate((rs_mid, ag.at[0], cs_mid, cn_mid, ag2.at[0])):
        wait_chips(buf, all_s.at[i])


def mix(step, tok_dev, place, start_ref, sp, gout, grow_ref, wo, out_ref):
    c = pl.program_id(0)
    at = c * step
    pairs = sp.shape[1]
    pos = start_ref[0] + at + lax.broadcasted_iota(jnp.int32, (step, NG), 0)
    one = jnp.where(pos == grow_ref[...], 1.0, 0.0)
    is_g = jnp.max(one, axis=-1, keepdims=True) > 0.5
    put = jnp.dot(one.astype(BF), gout[...], preferred_element_type=F32)
    own = jnp.concatenate(
        [
            jnp.concatenate([sp[place[c * (step // BLK) + i], p] for p in range(pairs)], axis=1)
            for i in range(step // BLK)
        ],
        axis=0,
    )
    att = jnp.where(is_g, put, own.astype(F32)).astype(BF)
    out_ref[...] = jnp.dot(att, wo[...], preferred_element_type=F32).astype(BF)


def body(n, tokens, w_query, w_key, w_value, w_out, rand_blocks, global_pos):
    tok_dev, width = tokens.shape
    nblk = tok_dev // BLK
    pairs = width // LANES
    cb = 256 if n <= 32 else 128
    rb = NG * width // (n * cb)
    ext = nblk + 2 + NFAR + NG // BLK
    dma = pltpu.SemaphoreType.DMA
    vm = pltpu.VMEM
    nc = n // 2
    both = vm((2, nc, rb, cb), BF)
    piece = vm((nc, rb, cb), BF)
    stat = vm((nc, 1, LANES), F32)
    keys = (3 + RAND) * BLK + NG
    big = vm((2, pairs // 2, 2 * BLK, keys), F32)
    small = vm((2, pairs // 2, 2 * BLK, LANES), F32)
    scratch = [
        vm((nblk, BLK, width), BF), vm((3, width, width), BF),
        vm((ext, 3, pairs, BLK, LANES), BF),
        vm((NG, width), BF), vm((NG, width), F32), vm((NG, tok_dev), BF),
        vm((NFAR, BLK, width), BF), vm((2 + NFAR, BLK, width), BF),
        vm((NFAR, 8, LANES), jnp.int32), vm((NFAR, 8, LANES), jnp.int32),
        pltpu.SMEM((nblk,), jnp.int32),
        both, piece, piece, piece, both, both, piece, piece, piece,
        vm((2, nc, 1, LANES), F32), stat, stat, stat, both,
        big, small, big, small,
        dma((4,)), dma((NFAR,)), dma((NFAR,)), dma((2 + NFAR,)), dma((2 + NFAR,)),
        dma((5,)), dma((5,)), dma((5,)), dma((5,)),
    ]
    anyspace = pl.BlockSpec(memory_space=pl.ANY)
    vmem = pl.BlockSpec(memory_space=pltpu.VMEM)
    smem = pl.BlockSpec(memory_space=pltpu.SMEM)
    grow = global_pos.reshape(1, NG)
    rbt = rand_blocks.T
    sp, gout, place = pl.pallas_call(
        functools.partial(attention, n),
        out_shape=(
            jax.ShapeDtypeStruct((nblk, pairs, BLK, LANES), BF),
            jax.ShapeDtypeStruct((NG, width), BF),
            jax.ShapeDtypeStruct((nblk,), jnp.int32),
        ),
        in_specs=[anyspace] * 4 + [vmem] * 2 + [smem],
        out_specs=(vmem, vmem, smem),
        scratch_shapes=scratch,
        compiler_params=pltpu.CompilerParams(
            collective_id=0, has_side_effects=True, vmem_limit_bytes=51 << 20
        ),
        name="attention",
    )(tokens.reshape(nblk, BLK, width), w_query, w_key, w_value, rbt, grow, rbt)
    step = 256
    start = (lax.axis_index("seq") * tok_dev).reshape(1).astype(jnp.int32)
    return pl.pallas_call(
        functools.partial(mix, step, tok_dev),
        grid=(tok_dev // step,),
        out_shape=jax.ShapeDtypeStruct((tok_dev, width), BF),
        in_specs=[smem, smem, vmem, vmem, vmem, vmem],
        out_specs=pl.BlockSpec((step, width), lambda i: (i, 0)),
        compiler_params=pltpu.CompilerParams(vmem_limit_bytes=32 << 20),
        name="mix",
    )(place, start, sp, gout, grow, w_out)


def solution(mesh):
    placed = (P("seq", None), P(), P(), P(), P(), P("seq", None), P())
    return jax.shard_map(
        functools.partial(body, mesh.shape["seq"]), mesh=mesh, in_specs=placed,
        out_specs=P("seq", None), check_vma=False,
    )
```

```python
import functools
import math

import jax
import jax.numpy as jnp
from jax import lax
from jax.experimental import pallas as pl
from jax.experimental.pallas import tpu as pltpu
from jax.sharding import PartitionSpec as P

HEADS = 16
HD = 64
BLK = 64
RAND = 3
NG = 128
FAR = 3
OFFSETS = tuple(range(-FAR, 0)) + tuple(range(1, FAR + 1))
NFAR = len(OFFSETS)
LANES = 128
EXP_SCALE = math.log2(math.e) / math.sqrt(HD)
SCORE_SCALE = 1.0 / math.sqrt(HD)
MESH = pl.DeviceIdType.MESH
BF = jnp.bfloat16
F32 = jnp.float32
NT = (((1,), (1,)), ((), ()))


def attention(
    n,
    tok_hbm, wq_hbm, wk_hbm, wv_hbm, rbv_ref, grow_ref, rb_ref,
    sp, gout, place,
    xt, wall, kv, xg, gf, sel, far, land,
    req_out, reqin, order,
    rs_out, rs_pair, rs_mid, rs_in, ag, cn_out, cn_pair, cn_mid, cn_in,
    cs_out, cs_pair, cs_mid, cs_in, ag2,
    sc, top, ex, inv, gsc, gtop,
    load_sem, req_s, req_r, edge_s, edge_r, one_s, one_r, all_s, all_r,
):
    nblk, _, width = tok_hbm.shape
    tok_dev = nblk * BLK
    me = lax.axis_index("seq")
    core, chip = lax.rem(me, 2), lax.div(me, 2)
    mate = me + 1 - 2 * core
    _, nc, rb, cb = ag.shape
    ncg = width // cb
    hpb = cb // HD
    pairs = width // LANES
    right0 = nblk + 1
    far0 = nblk + 2
    glob0 = far0 + NFAR
    gblk = NG // BLK

    loads = [
        pltpu.make_async_copy(src, dst, load_sem.at[i])
        for i, (src, dst) in enumerate(
            (
                (tok_hbm, xt), (wk_hbm, wall.at[0]), (wv_hbm, wall.at[1]),
                (wq_hbm, wall.at[2]),
            )
        )
    ]
    for cp in loads:
        cp.start()

    land[...] = jnp.zeros(land.shape, BF)
    reqin[...] = jnp.zeros(reqin.shape, jnp.int32)
    base = rbv_ref[RAND - 1:RAND, :] - me * nblk
    for i, o in enumerate(OFFSETS):
        loc = base - o * nblk
        loc = jnp.where((loc >= 0) & (loc < nblk), loc, 0)
        want = jnp.sum(loc, axis=1, keepdims=True)
        req_out[i] = jnp.broadcast_to(want, (8, LANES))

    def exists(o):
        return me + o >= 0 if o < 0 else me + o < n

    barrier = pltpu.get_barrier_semaphore()
    other = me - 1 + 2 * core

    def greet(device):
        pl.semaphore_signal(barrier, inc=1, device_id=(device,), device_id_type=MESH)

    def greet_chip(o, c):
        greet(2 * lax.rem(chip + o, nc) + core)
        return c

    lax.fori_loop(1, nc, greet_chip, 0)
    greet(mate)
    there = ((other >= 0) & (other < n), other), (exists(-FAR), me - FAR), (exists(FAR), me + FAR)
    for ok, device in there:
        @pl.when(ok)
        def _():
            greet(device)

    def to_chips(src, dst, i):
        def one(o, c):
            peer = lax.rem(chip + o, nc)
            pltpu.make_async_remote_copy(
                src_ref=src(peer), dst_ref=dst, send_sem=all_s.at[i], recv_sem=all_r.at[i],
                device_id=(2 * peer + core,), device_id_type=MESH,
            ).start()
            return c

        lax.fori_loop(1, nc, one, 0)

    def wait_chips(buf, sem):
        part = buf.at[pl.ds(0, nc - 1)]
        pltpu.make_async_copy(part, part, sem).wait()

    def to_mate(src, dst, i):
        return pltpu.make_async_remote_copy(
            src_ref=src, dst_ref=dst, send_sem=one_s.at[i], recv_sem=one_r.at[i],
            device_id=(mate,), device_id_type=MESH,
        )

    rs_mate = to_mate(rs_out.at[1 - core], rs_pair, 0)
    ag_mate = to_mate(ag.at[core], ag.at[core], 1)
    cs_mate = to_mate(cs_out.at[1 - core], cs_pair, 2)
    cn_mate = to_mate(cn_out.at[1 - core], cn_pair, 3)
    ag2_mate = to_mate(ag2.at[core], ag2.at[core], 4)

    def req_copy(i):
        return pltpu.make_async_remote_copy(
            src_ref=req_out.at[i], dst_ref=reqin.at[i], send_sem=req_s.at[i],
            recv_sem=req_r.at[i], device_id=(me + OFFSETS[i],), device_id_type=MESH,
        )

    def far_copy(i):
        return pltpu.make_async_remote_copy(
            src_ref=far.at[i],
            dst_ref=land.at[2 + i],
            send_sem=edge_s.at[2 + i], recv_sem=edge_r.at[2 + i],
            device_id=(me - OFFSETS[i],), device_id_type=MESH,
        )

    def halo_copy(side):
        src, dst, dev = (0, 1, me - 1) if side == 0 else (nblk - 1, 0, me + 1)
        return pltpu.make_async_remote_copy(
            src_ref=xt.at[src], dst_ref=land.at[dst],
            send_sem=edge_s.at[side], recv_sem=edge_r.at[side],
            device_id=(dev,), device_id_type=MESH,
        )

    diag = lax.broadcasted_iota(jnp.int32, (NG, NG), 0) == lax.broadcasted_iota(
        jnp.int32, (NG, NG), 1
    )
    gcol = jnp.sum(
        jnp.where(diag, (grow_ref[...] - me * tok_dev).astype(F32), 0.0), axis=1, keepdims=True
    )
    hit = gcol == lax.broadcasted_iota(jnp.int32, (NG, tok_dev), 1).astype(F32)
    sel[...] = jnp.where(hit, 1.0, 0.0).astype(BF)

    loads[0].wait()
    picked = jnp.dot(sel[...], xt[...].reshape(tok_dev, width), preferred_element_type=F32)
    if rb % 16 == 0:
        picked = picked.astype(BF)
        for d in range(n):
            r, c = (d // ncg) * rb, (d % ncg) * cb
            rs_out[d % 2, d // 2] = picked[r:r + rb, c:c + cb]
    else:
        gf[...] = picked
        for d in range(n):
            r, c = (d // ncg) * rb, (d % ncg) * cb
            rs_out[d % 2, d // 2] = gf[r:r + rb, c:c + cb].astype(BF)
    def begin():
        pl.semaphore_wait(barrier, nc + sum(jnp.where(ok, 1, 0) for ok, _ in there))
        rs_mate.start()
        for i, o in enumerate(OFFSETS):
            @pl.when(exists(o))
            def _():
                req_copy(i).start()


    def reduce_pair():
        rs_mate.wait_recv()
        rs_mid[...] = rs_out[core] + rs_pair[...]
        to_chips(lambda p: rs_mid.at[p], rs_in.at[chip], 0)
        rs_in[chip] = rs_mid[chip]

    def gather():
        wait_chips(rs_in, all_r.at[0])
        ag[core, chip] = jnp.sum(rs_in[...].astype(F32), axis=0).astype(BF)
        to_chips(lambda p: ag.at[core, chip], ag.at[core, chip], 1)

    def send_edges():
        for side, o in ((0, -1), (1, 1)):
            @pl.when(exists(o))
            def _():
                halo_copy(side).start()
        for i, o in enumerate(OFFSETS):
            @pl.when(exists(-o))
            def _():
                req_copy(i).wait_recv()
        for i, o in enumerate(OFFSETS):
            want = jnp.minimum(jnp.maximum(reqin[i, 0, 0], 0), nblk - 1)
            far[i] = xt[want]

            @pl.when(exists(-o))
            def _():
                far_copy(i).start()

    def gather_pair():
        wait_chips(ag.at[0], all_r.at[1])
        ag_mate.start()

    step = 512
    parts = tok_dev // step

    def project(c, carry):
        for i in range(3):
            @pl.when(c == i * parts)
            def _():
                loads[1 + i].wait()

        for at, act in ((1, begin), (2, reduce_pair), (4, gather), (4, send_edges)):
            @pl.when(c == at)
            def _():
                act()

        which, part = lax.div(c, parts), lax.rem(c, parts)
        rows = xt[pl.ds(part * (step // BLK), step // BLK)].reshape(step, width)
        val = jnp.dot(rows, wall[which], preferred_element_type=F32).astype(BF)
        for p in range(pairs):
            kv[pl.ds(1 + part * (step // BLK), step // BLK), which, p] = val[
                :, p * LANES:(p + 1) * LANES
            ].reshape(step // BLK, BLK, LANES)
        return carry

    lax.fori_loop(0, 3 * parts, project, 0)
    gather_pair()

    lates = []
    for b in range(1, nblk - 1):
        r = rb_ref[RAND - 1, b] - me * nblk
        lates.append(jnp.where((r >= 0) & (r < nblk), 0, 1))
    early = nblk - 2 - sum(lates)
    seen = jnp.int32(0)
    spots = []
    for b in range(1, nblk - 1):
        late = lates[b - 1]
        spots.append(jnp.where(late == 1, early + seen, b - 1 - seen))
        seen = seen + late
        place[b] = spots[b - 1]
    for t in range(nblk - 2):
        order[t] = sum(jnp.where(spots[b - 1] == t, b, 0) for b in range(1, nblk - 1))
    place[0] = nblk - 2
    place[nblk - 1] = nblk - 1

    ag_mate.wait_recv()
    for d in range(n):
        r, c = (d // ncg) * rb, (d % ncg) * cb
        if rb % 16 == 0:
            xg[r:r + rb, c:c + cb] = ag[d % 2, d // 2]
        else:
            gf[r:r + rb, c:c + cb] = ag[d % 2, d // 2].astype(F32)
    if rb % 16:
        xg[...] = gf[...].astype(BF)

    def project_global(i, carry):
        val = jnp.dot(xg[...], wall[i], preferred_element_type=F32).astype(BF)
        for p in range(pairs):
            kv[glob0:glob0 + gblk, i, p] = val[:, p * LANES:(p + 1) * LANES].reshape(
                gblk, BLK, LANES
            )
        return carry

    lax.fori_loop(0, 3, project_global, 0)

    lane = lax.broadcasted_iota(jnp.int32, (1, LANES), 1)
    islo = lane < HD
    halves = (jnp.where(islo, 1.0, 0.0).astype(BF), jnp.where(islo, 0.0, 1.0).astype(BF))
    wide_row = LANES // rb
    lane_f = jnp.bitwise_and(lane, wide_row - 1)
    own_row = lax.shift_right_logical(
        lax.broadcasted_iota(jnp.int32, (rb, LANES), 1), wide_row.bit_length() - 1
    ) == lax.broadcasted_iota(jnp.int32, (rb, LANES), 0)
    head_of = jnp.where(
        jnp.bitwise_and(lax.broadcasted_iota(jnp.int32, (LANES, cb), 0), wide_row - 1)
        == lax.shift_right_logical(lax.broadcasted_iota(jnp.int32, (LANES, cb), 1), 6),
        1.0, 0.0,
    )

    def flat(x):
        return jnp.sum(jnp.where(own_row, x, 0.0), axis=0, keepdims=True)

    def spread(x):
        rows = [jnp.where(own_row, x[i:i + 1], 0.0) for i in range(nc)]
        return jnp.dot(
            jnp.concatenate(rows, axis=0), head_of, preferred_element_type=F32,
            precision=lax.Precision.HIGHEST,
        )

    def stacked(x):
        return jnp.concatenate([x * m for m in halves], axis=0)

    def with_ones(x):
        return jnp.concatenate([x, jnp.ones(x.shape, BF)], axis=1)

    per = cb // LANES

    def global_scores(cg):
        for j in range(per):
            p = cg * per + j
            s = lax.dot_general(
                stacked(kv[glob0:glob0 + gblk, 2, p].reshape(NG, LANES)),
                kv[1:1 + nblk, 0, p].reshape(tok_dev, LANES), NT,
                preferred_element_type=F32,
            )
            gsc[cg % 2, j] = s
            gtop[cg % 2, j] = jnp.broadcast_to(
                jnp.max(s, axis=-1, keepdims=True), (2 * NG, LANES)
            )

    def global_sums(cg):
        nums, stat = [], jnp.zeros((NG, LANES), F32)
        for j in range(per):
            p = cg * per + j
            m = gtop[cg % 2, j]
            shift = jnp.concatenate([m] * (tok_dev // LANES), axis=1)
            e = jnp.exp2((gsc[cg % 2, j] - shift) * EXP_SCALE).astype(BF)
            x = jnp.dot(
                e, with_ones(kv[1:1 + nblk, 1, p].reshape(tok_dev, LANES)),
                preferred_element_type=F32,
            )
            nums.append(jnp.where(islo, x[:NG, :LANES], x[NG:, :LANES]).astype(BF))
            m = m * SCORE_SCALE
            for h in range(2):
                rows = slice(h * NG, (h + 1) * NG)
                stat = jnp.where(lane_f == 2 * j + h, m[rows], stat)
                stat = jnp.where(lane_f == hpb + 2 * j + h, x[rows, LANES:], stat)
        num = jnp.concatenate(nums, axis=1) if per > 1 else nums[0]
        for rg in range(NG // rb):
            d = rg * ncg + cg
            cn_out[d % 2, d // 2] = num[rg * rb:(rg + 1) * rb]
            cs_out[d % 2, d // 2] = flat(stat[rg * rb:(rg + 1) * rb])

    global_scores(0)
    for cg in range(ncg):
        global_sums(cg)
        if cg + 1 < ncg:
            global_scores(cg + 1)
    cs_mate.start()
    cn_mate.start()

    def merge_pair():
        cs_mate.wait_recv()
        cn_mate.wait_recv()
        a, b = cs_out[core].reshape(nc, LANES), cs_pair[...].reshape(nc, LANES)
        m = jnp.maximum(a, b)
        ea, eb = jnp.exp(a - m), jnp.exp(b - m)
        t = a * pltpu.roll(ea, hpb, 1) + b * pltpu.roll(eb, hpb, 1)
        cs_mid[...] = jnp.where(lane_f < hpb, m, t).reshape(nc, 1, LANES)
        clean = lane_f < hpb
        fa, fb = spread(jnp.where(clean, ea, 0.0)), spread(jnp.where(clean, eb, 0.0))
        for i in range(nc):
            rows = slice(i * rb, (i + 1) * rb)
            cn_mid[i] = (
                cn_out[core, i].astype(F32) * fa[rows] + cn_pair[i].astype(F32) * fb[rows]
            ).astype(BF)
        to_chips(lambda p: cs_mid.at[p], cs_in.at[chip], 2)
        to_chips(lambda p: cn_mid.at[p], cn_in.at[chip], 3)
        cs_in[chip] = cs_mid[chip]
        cn_in[chip] = cn_mid[chip]

    def choose(b):
        picks = []
        for r in range(RAND):
            rel = rb_ref[r, b] - me * nblk
            dev = lax.div(rel + FAR * nblk, nblk)
            slot = jnp.where(dev < FAR, dev, dev - 1)
            pick = jnp.where(dev == FAR, rel + 1, far0 + slot)
            picks.append(jnp.minimum(jnp.maximum(pick, 0), far0 + NFAR - 1))
        return picks

    def rows_of(which, p, b, picks):
        return jnp.concatenate(
            [kv[b + i, which, p] for i in range(3)]
            + [kv[i, which, p] for i in picks]
            + [kv[glob0 + i, which, p] for i in range(gblk)],
            axis=0,
        )

    half = pairs // 2
    nsub = (3 + RAND) * BLK // LANES + NG // LANES

    def wide(x):
        return jnp.concatenate([x] * nsub, axis=1)

    def scores(g, blk):
        t, b, picks, bias = blk
        for j in range(half):
            p = g * half + j
            s = lax.dot_general(
                stacked(kv[1 + b, 2, p]), rows_of(0, p, b, picks), NT, preferred_element_type=F32
            )
            if bias is not None:
                s = s + bias
            sc[g, j] = s
            top[g, j] = jnp.broadcast_to(
                jnp.max(s, axis=-1, keepdims=True), (2 * BLK, LANES)
            )

    def expo(g):
        for j in range(half):
            e = jnp.exp2((sc[g, j] - wide(top[g, j])) * EXP_SCALE)
            ex[g, j] = e
            inv[g, j] = jnp.broadcast_to(
                1.0 / jnp.sum(e, axis=-1, keepdims=True), (2 * BLK, LANES)
            )

    def weigh(g, blk):
        t, b, picks, _ = blk
        for j in range(0, half, 2):
            p = g * half + j
            w = jnp.concatenate(
                [(ex[g, j + i] * wide(inv[g, j + i])).astype(BF) for i in range(2)], axis=0
            )
            x = jnp.dot(
                w,
                jnp.concatenate([rows_of(1, p + i, b, picks) for i in range(2)], axis=1),
                preferred_element_type=F32,
            )
            for i in range(2):
                y = x[i * 2 * BLK:(i + 1) * 2 * BLK, i * LANES:(i + 1) * LANES]
                sp[t, p + i] = jnp.where(islo, y[:BLK], y[BLK:]).astype(BF)

    def attend(before, blocks):
        seq = [before] + blocks
        for i, blk in enumerate(blocks):
            expo(1)
            scores(0, blk)
            weigh(0, seq[i])
            expo(0)
            scores(1, blk)
            weigh(1, seq[i])

    def block_at(t, b, bias=None):
        return t, b, choose(b), bias

    def between():
        wait_chips(cs_in, all_r.at[2])
        wait_chips(cn_in, all_r.at[3])
        stat = cs_in[...].reshape(nc, LANES)
        e = jnp.exp(stat - jnp.max(stat, axis=0, keepdims=True))
        den = jnp.sum(pltpu.roll(stat, LANES - hpb, 1) * e, axis=0, keepdims=True)
        fac = spread(jnp.where(lane_f < hpb, e / den, 0.0))
        num = cn_in[0].astype(F32) * fac[0:rb]
        for i in range(1, nc):
            num = num + cn_in[i].astype(F32) * fac[i * rb:(i + 1) * rb]
        ag2[core, chip] = num.astype(BF)
        to_chips(lambda p: ag2.at[core, chip], ag2.at[core, chip], 4)

        for side, o in ((0, 1), (1, -1)):
            @pl.when(exists(o))
            def _():
                halo_copy(side).wait_recv()
        for i, o in enumerate(OFFSETS):
            @pl.when(exists(o))
            def _():
                far_copy(i).wait_recv()
        def project_edges(i, carry):
            rows = land[...].reshape((2 + NFAR) * BLK, width)
            val = jnp.dot(rows, wall[i], preferred_element_type=F32).astype(BF)
            for p in range(pairs):
                x = val[:, p * LANES:(p + 1) * LANES].reshape(2 + NFAR, BLK, LANES)
                kv[0, i, p] = x[0]
                kv[right0:glob0, i, p] = x[1:]
            return carry

        lax.fori_loop(0, 2, project_edges, 0)

    def two(i, carry):
        @pl.when(i == 1)
        def _():
            merge_pair()

        @pl.when(i == nblk // 4)
        def _():
            between()

        @pl.when(i == nblk // 4 + 2)
        def _():
            wait_chips(ag2.at[0], all_r.at[4])
            ag2_mate.start()

        prev = jnp.maximum(2 * i - 1, 0)
        attend(
            block_at(prev, order[prev]),
            [block_at(2 * i + j, order[2 * i + j]) for j in range(2)],
        )
        return carry

    lax.fori_loop(0, nblk // 2 - 1, two, 0)
    key_col = lax.broadcasted_iota(jnp.int32, (1, (3 + RAND) * BLK + NG), 1)
    lead = jnp.where(me == 0, BLK, 0)
    tail = jnp.where(me == n - 1, 2 * BLK, 3 * BLK)
    first = jnp.where(key_col < lead, -1e30, 0.0)
    last = jnp.where((key_col >= tail) & (key_col < 3 * BLK), -1e30, 0.0)
    end = block_at(nblk - 1, nblk - 1, last)
    attend(block_at(nblk - 3, order[nblk - 3]), [block_at(nblk - 2, 0, first), end])
    expo(1)
    weigh(0, end)
    weigh(1, end)

    ag2_mate.wait_recv()
    for d in range(n):
        r, c = (d // ncg) * rb, (d % ncg) * cb
        if rb % 16 == 0:
            gout[r:r + rb, c:c + cb] = ag2[d % 2, d // 2]
        else:
            gf[r:r + rb, c:c + cb] = ag2[d % 2, d // 2].astype(F32)
    if rb % 16:
        gout[...] = gf[...].astype(BF)

    for i, o in enumerate(OFFSETS):
        @pl.when(exists(o))
        def _():
            req_copy(i).wait_send()

        @pl.when(exists(-o))
        def _():
            far_copy(i).wait_send()
    for side, o in ((0, -1), (1, 1)):
        @pl.when(exists(o))
        def _():
            halo_copy(side).wait_send()
    for cp in (rs_mate, ag_mate, cs_mate, cn_mate, ag2_mate):
        cp.wait_send()
    for i, buf in enumerate((rs_mid, ag.at[0], cs_mid, cn_mid, ag2.at[0])):
        wait_chips(buf, all_s.at[i])


def mix(step, tok_dev, place, start_ref, sp, gout, grow_ref, wo, out_ref):
    c = pl.program_id(0)
    at = c * step
    pairs = sp.shape[1]
    pos = start_ref[0] + at + lax.broadcasted_iota(jnp.int32, (step, NG), 0)
    one = jnp.where(pos == grow_ref[...], 1.0, 0.0)
    is_g = jnp.max(one, axis=-1, keepdims=True) > 0.5
    put = jnp.dot(one.astype(BF), gout[...], preferred_element_type=F32)
    own = jnp.concatenate(
        [
            jnp.concatenate([sp[place[c * (step // BLK) + i], p] for p in range(pairs)], axis=1)
            for i in range(step // BLK)
        ],
        axis=0,
    )
    att = jnp.where(is_g, put, own.astype(F32)).astype(BF)
    out_ref[...] = jnp.dot(att, wo[...], preferred_element_type=F32).astype(BF)


def body(n, tokens, w_query, w_key, w_value, w_out, rand_blocks, global_pos):
    tok_dev, width = tokens.shape
    nblk = tok_dev // BLK
    pairs = width // LANES
    cb = 256 if n <= 32 else 128
    rb = NG * width // (n * cb)
    ext = nblk + 2 + NFAR + NG // BLK
    dma = pltpu.SemaphoreType.DMA
    vm = pltpu.VMEM
    nc = n // 2
    both = vm((2, nc, rb, cb), BF)
    piece = vm((nc, rb, cb), BF)
    stat = vm((nc, 1, LANES), F32)
    keys = (3 + RAND) * BLK + NG
    big = vm((2, pairs // 2, 2 * BLK, keys), F32)
    small = vm((2, pairs // 2, 2 * BLK, LANES), F32)
    scratch = [
        vm((nblk, BLK, width), BF), vm((3, width, width), BF),
        vm((ext, 3, pairs, BLK, LANES), BF),
        vm((NG, width), BF), vm((NG, width), F32), vm((NG, tok_dev), BF),
        vm((NFAR, BLK, width), BF), vm((2 + NFAR, BLK, width), BF),
        vm((NFAR, 8, LANES), jnp.int32), vm((NFAR, 8, LANES), jnp.int32),
        pltpu.SMEM((nblk,), jnp.int32),
        both, piece, piece, piece, both, both, piece, piece, piece,
        vm((2, nc, 1, LANES), F32), stat, stat, stat, both,
        big, small, big, small,
        vm((2, cb // LANES, 2 * NG, tok_dev), F32), vm((2, cb // LANES, 2 * NG, LANES), F32),
        dma((4,)), dma((NFAR,)), dma((NFAR,)), dma((2 + NFAR,)), dma((2 + NFAR,)),
        dma((5,)), dma((5,)), dma((5,)), dma((5,)),
    ]
    anyspace = pl.BlockSpec(memory_space=pl.ANY)
    vmem = pl.BlockSpec(memory_space=pltpu.VMEM)
    smem = pl.BlockSpec(memory_space=pltpu.SMEM)
    grow = global_pos.reshape(1, NG)
    rbt = rand_blocks.T
    sp, gout, place = pl.pallas_call(
        functools.partial(attention, n),
        out_shape=(
            jax.ShapeDtypeStruct((nblk, pairs, BLK, LANES), BF),
            jax.ShapeDtypeStruct((NG, width), BF),
            jax.ShapeDtypeStruct((nblk,), jnp.int32),
        ),
        in_specs=[anyspace] * 4 + [vmem] * 2 + [smem],
        out_specs=(vmem, vmem, smem),
        scratch_shapes=scratch,
        compiler_params=pltpu.CompilerParams(
            collective_id=0, has_side_effects=True, vmem_limit_bytes=51 << 20
        ),
        name="attention",
    )(tokens.reshape(nblk, BLK, width), w_query, w_key, w_value, rbt, grow, rbt)
    step = 256
    start = (lax.axis_index("seq") * tok_dev).reshape(1).astype(jnp.int32)
    return pl.pallas_call(
        functools.partial(mix, step, tok_dev),
        grid=(tok_dev // step,),
        out_shape=jax.ShapeDtypeStruct((tok_dev, width), BF),
        in_specs=[smem, smem, vmem, vmem, vmem, vmem],
        out_specs=pl.BlockSpec((step, width), lambda i: (i, 0)),
        compiler_params=pltpu.CompilerParams(vmem_limit_bytes=32 << 20),
        name="mix",
    )(place, start, sp, gout, grow, w_out)


def solution(mesh):
    placed = (P("seq", None), P(), P(), P(), P(), P("seq", None), P())
    return jax.shard_map(
        functools.partial(body, mesh.shape["seq"]), mesh=mesh, in_specs=placed,
        out_specs=P("seq", None), check_vma=False,
    )
```

```python
import functools
import math

import jax
import jax.numpy as jnp
from jax import lax
from jax.experimental import pallas as pl
from jax.experimental.pallas import tpu as pltpu
from jax.sharding import PartitionSpec as P

HEADS = 16
HD = 64
BLK = 64
RAND = 3
NG = 128
FAR = 3
OFFSETS = tuple(range(-FAR, 0)) + tuple(range(1, FAR + 1))
NFAR = len(OFFSETS)
LANES = 128
EXP_SCALE = math.log2(math.e) / math.sqrt(HD)
SCORE_SCALE = 1.0 / math.sqrt(HD)
MESH = pl.DeviceIdType.MESH
BF = jnp.bfloat16
F32 = jnp.float32
NT = (((1,), (1,)), ((), ()))


def attention(
    n,
    tok_hbm, wq_hbm, wk_hbm, wv_hbm, rbv_ref, grow_ref, rb_ref,
    sp, gout, place,
    xt, wall, kv, xg, gf, sel, far, land,
    req_out, reqin, order,
    rs_out, rs_pair, rs_mid, rs_in, ag, cn_out, cn_pair, cn_mid, cn_in,
    cs_out, cs_pair, cs_mid, cs_in, ag2,
    sc, top, ex, inv, gsc, gtop,
    load_sem, req_s, req_r, edge_s, edge_r, one_s, one_r, all_s, all_r,
):
    nblk, _, width = tok_hbm.shape
    tok_dev = nblk * BLK
    me = lax.axis_index("seq")
    core, chip = lax.rem(me, 2), lax.div(me, 2)
    mate = me + 1 - 2 * core
    _, nc, rb, cb = ag.shape
    ncg = width // cb
    hpb = cb // HD
    pairs = width // LANES
    right0 = nblk + 1
    far0 = nblk + 2
    glob0 = far0 + NFAR
    gblk = NG // BLK

    loads = [
        pltpu.make_async_copy(src, dst, load_sem.at[i])
        for i, (src, dst) in enumerate(
            (
                (tok_hbm, xt), (wk_hbm, wall.at[0]), (wv_hbm, wall.at[1]),
                (wq_hbm, wall.at[2]),
            )
        )
    ]
    for cp in loads:
        cp.start()

    land[...] = jnp.zeros(land.shape, BF)
    reqin[...] = jnp.zeros(reqin.shape, jnp.int32)
    base = rbv_ref[RAND - 1:RAND, :] - me * nblk
    for i, o in enumerate(OFFSETS):
        loc = base - o * nblk
        loc = jnp.where((loc >= 0) & (loc < nblk), loc, 0)
        want = jnp.sum(loc, axis=1, keepdims=True)
        req_out[i] = jnp.broadcast_to(want, (8, LANES))

    def exists(o):
        return me + o >= 0 if o < 0 else me + o < n

    barrier = pltpu.get_barrier_semaphore()
    other = me - 1 + 2 * core

    def greet(device):
        pl.semaphore_signal(barrier, inc=1, device_id=(device,), device_id_type=MESH)

    def greet_chip(o, c):
        greet(2 * lax.rem(chip + o, nc) + core)
        return c

    lax.fori_loop(1, nc, greet_chip, 0)
    greet(mate)
    there = ((other >= 0) & (other < n), other), (exists(-FAR), me - FAR), (exists(FAR), me + FAR)
    for ok, device in there:
        @pl.when(ok)
        def _():
            greet(device)

    def to_chips(src, dst, i):
        def one(o, c):
            peer = lax.rem(chip + o, nc)
            pltpu.make_async_remote_copy(
                src_ref=src(peer), dst_ref=dst, send_sem=all_s.at[i], recv_sem=all_r.at[i],
                device_id=(2 * peer + core,), device_id_type=MESH,
            ).start()
            return c

        lax.fori_loop(1, nc, one, 0)

    def wait_chips(buf, sem):
        part = buf.at[pl.ds(0, nc - 1)]
        pltpu.make_async_copy(part, part, sem).wait()

    def to_mate(src, dst, i):
        return pltpu.make_async_remote_copy(
            src_ref=src, dst_ref=dst, send_sem=one_s.at[i], recv_sem=one_r.at[i],
            device_id=(mate,), device_id_type=MESH,
        )

    rs_mate = to_mate(rs_out.at[1 - core], rs_pair, 0)
    ag_mate = to_mate(ag.at[core], ag.at[core], 1)
    cs_mate = to_mate(cs_out.at[1 - core], cs_pair, 2)
    cn_mate = to_mate(cn_out.at[1 - core], cn_pair, 3)
    ag2_mate = to_mate(ag2.at[core], ag2.at[core], 4)

    def req_copy(i):
        return pltpu.make_async_remote_copy(
            src_ref=req_out.at[i], dst_ref=reqin.at[i], send_sem=req_s.at[i],
            recv_sem=req_r.at[i], device_id=(me + OFFSETS[i],), device_id_type=MESH,
        )

    def far_copy(i):
        return pltpu.make_async_remote_copy(
            src_ref=far.at[i],
            dst_ref=land.at[2 + i],
            send_sem=edge_s.at[2 + i], recv_sem=edge_r.at[2 + i],
            device_id=(me - OFFSETS[i],), device_id_type=MESH,
        )

    def halo_copy(side):
        src, dst, dev = (0, 1, me - 1) if side == 0 else (nblk - 1, 0, me + 1)
        return pltpu.make_async_remote_copy(
            src_ref=xt.at[src], dst_ref=land.at[dst],
            send_sem=edge_s.at[side], recv_sem=edge_r.at[side],
            device_id=(dev,), device_id_type=MESH,
        )

    diag = lax.broadcasted_iota(jnp.int32, (NG, NG), 0) == lax.broadcasted_iota(
        jnp.int32, (NG, NG), 1
    )
    gcol = jnp.sum(
        jnp.where(diag, (grow_ref[...] - me * tok_dev).astype(F32), 0.0), axis=1, keepdims=True
    )
    hit = gcol == lax.broadcasted_iota(jnp.int32, (NG, tok_dev), 1).astype(F32)
    sel[...] = jnp.where(hit, 1.0, 0.0).astype(BF)

    loads[0].wait()
    picked = jnp.dot(sel[...], xt[...].reshape(tok_dev, width), preferred_element_type=F32)
    if rb % 16 == 0:
        picked = picked.astype(BF)
        for d in range(n):
            r, c = (d // ncg) * rb, (d % ncg) * cb
            rs_out[d % 2, d // 2] = picked[r:r + rb, c:c + cb]
    else:
        gf[...] = picked
        for d in range(n):
            r, c = (d // ncg) * rb, (d % ncg) * cb
            rs_out[d % 2, d // 2] = gf[r:r + rb, c:c + cb].astype(BF)
    pl.semaphore_wait(barrier, nc + sum(jnp.where(ok, 1, 0) for ok, _ in there))
    rs_mate.start()
    for i, o in enumerate(OFFSETS):
        @pl.when(exists(o))
        def _():
            req_copy(i).start()


    def reduce_pair():
        rs_mate.wait_recv()
        rs_mid[...] = rs_out[core] + rs_pair[...]
        to_chips(lambda p: rs_mid.at[p], rs_in.at[chip], 0)
        rs_in[chip] = rs_mid[chip]

    def gather():
        wait_chips(rs_in, all_r.at[0])
        ag[core, chip] = jnp.sum(rs_in[...].astype(F32), axis=0).astype(BF)
        to_chips(lambda p: ag.at[core, chip], ag.at[core, chip], 1)

    def send_edges():
        for side, o in ((0, -1), (1, 1)):
            @pl.when(exists(o))
            def _():
                halo_copy(side).start()
        for i, o in enumerate(OFFSETS):
            @pl.when(exists(-o))
            def _():
                req_copy(i).wait_recv()
        for i, o in enumerate(OFFSETS):
            want = jnp.minimum(jnp.maximum(reqin[i, 0, 0], 0), nblk - 1)
            far[i] = xt[want]

            @pl.when(exists(-o))
            def _():
                far_copy(i).start()

    def gather_pair():
        wait_chips(ag.at[0], all_r.at[1])
        ag_mate.start()

    step = 512
    parts = tok_dev // step

    def project(c, carry):
        for i in range(3):
            @pl.when(c == i * parts)
            def _():
                loads[1 + i].wait()

        for at, act in ((1, reduce_pair), (3, gather), (3, send_edges), (5, gather_pair)):
            @pl.when(c == at)
            def _():
                act()

        which, part = lax.div(c, parts), lax.rem(c, parts)
        rows = xt[pl.ds(part * (step // BLK), step // BLK)].reshape(step, width)
        val = jnp.dot(rows, wall[which], preferred_element_type=F32).astype(BF)
        for p in range(pairs):
            kv[pl.ds(1 + part * (step // BLK), step // BLK), which, p] = val[
                :, p * LANES:(p + 1) * LANES
            ].reshape(step // BLK, BLK, LANES)
        return carry

    lax.fori_loop(0, 3 * parts, project, 0)

    lates = []
    for b in range(1, nblk - 1):
        r = rb_ref[RAND - 1, b] - me * nblk
        lates.append(jnp.where((r >= 0) & (r < nblk), 0, 1))
    early = nblk - 2 - sum(lates)
    seen = jnp.int32(0)
    spots = []
    for b in range(1, nblk - 1):
        late = lates[b - 1]
        spots.append(jnp.where(late == 1, early + seen, b - 1 - seen))
        seen = seen + late
        place[b] = spots[b - 1]
    for t in range(nblk - 2):
        order[t] = sum(jnp.where(spots[b - 1] == t, b, 0) for b in range(1, nblk - 1))
    place[0] = nblk - 2
    place[nblk - 1] = nblk - 1

    ag_mate.wait_recv()
    for d in range(n):
        r, c = (d // ncg) * rb, (d % ncg) * cb
        if rb % 16 == 0:
            xg[r:r + rb, c:c + cb] = ag[d % 2, d // 2]
        else:
            gf[r:r + rb, c:c + cb] = ag[d % 2, d // 2].astype(F32)
    if rb % 16:
        xg[...] = gf[...].astype(BF)

    def project_global(i, carry):
        val = jnp.dot(xg[...], wall[i], preferred_element_type=F32).astype(BF)
        for p in range(pairs):
            kv[glob0:glob0 + gblk, i, p] = val[:, p * LANES:(p + 1) * LANES].reshape(
                gblk, BLK, LANES
            )
        return carry

    lax.fori_loop(0, 3, project_global, 0)

    lane = lax.broadcasted_iota(jnp.int32, (1, LANES), 1)
    islo = lane < HD
    halves = (jnp.where(islo, 1.0, 0.0).astype(BF), jnp.where(islo, 0.0, 1.0).astype(BF))
    wide_row = LANES // rb
    lane_f = jnp.bitwise_and(lane, wide_row - 1)
    own_row = lax.shift_right_logical(
        lax.broadcasted_iota(jnp.int32, (rb, LANES), 1), wide_row.bit_length() - 1
    ) == lax.broadcasted_iota(jnp.int32, (rb, LANES), 0)
    head_of = jnp.where(
        jnp.bitwise_and(lax.broadcasted_iota(jnp.int32, (LANES, cb), 0), wide_row - 1)
        == lax.shift_right_logical(lax.broadcasted_iota(jnp.int32, (LANES, cb), 1), 6),
        1.0, 0.0,
    )

    def flat(x):
        return jnp.sum(jnp.where(own_row, x, 0.0), axis=0, keepdims=True)

    def spread(x):
        rows = [jnp.where(own_row, x[i:i + 1], 0.0) for i in range(nc)]
        return jnp.dot(
            jnp.concatenate(rows, axis=0), head_of, preferred_element_type=F32,
            precision=lax.Precision.HIGHEST,
        )

    def stacked(x):
        return jnp.concatenate([x * m for m in halves], axis=0)

    def with_ones(x):
        return jnp.concatenate([x, jnp.ones(x.shape, BF)], axis=1)

    per = cb // LANES

    def global_scores(cg):
        for j in range(per):
            p = cg * per + j
            s = lax.dot_general(
                stacked(kv[glob0:glob0 + gblk, 2, p].reshape(NG, LANES)),
                kv[1:1 + nblk, 0, p].reshape(tok_dev, LANES), NT,
                preferred_element_type=F32,
            )
            gsc[cg % 2, j] = s
            gtop[cg % 2, j] = jnp.broadcast_to(
                jnp.max(s, axis=-1, keepdims=True), (2 * NG, LANES)
            )

    def global_sums(cg):
        nums, stat = [], jnp.zeros((NG, LANES), F32)
        for j in range(per):
            p = cg * per + j
            m = gtop[cg % 2, j]
            shift = jnp.concatenate([m] * (tok_dev // LANES), axis=1)
            e = jnp.exp2((gsc[cg % 2, j] - shift) * EXP_SCALE).astype(BF)
            x = jnp.dot(
                e, with_ones(kv[1:1 + nblk, 1, p].reshape(tok_dev, LANES)),
                preferred_element_type=F32,
            )
            nums.append(jnp.where(islo, x[:NG, :LANES], x[NG:, :LANES]).astype(BF))
            m = m * SCORE_SCALE
            for h in range(2):
                rows = slice(h * NG, (h + 1) * NG)
                stat = jnp.where(lane_f == 2 * j + h, m[rows], stat)
                stat = jnp.where(lane_f == hpb + 2 * j + h, x[rows, LANES:], stat)
        num = jnp.concatenate(nums, axis=1) if per > 1 else nums[0]
        for rg in range(NG // rb):
            d = rg * ncg + cg
            cn_out[d % 2, d // 2] = num[rg * rb:(rg + 1) * rb]
            cs_out[d % 2, d // 2] = flat(stat[rg * rb:(rg + 1) * rb])

    global_scores(0)
    for cg in range(ncg):
        global_sums(cg)
        if cg + 1 < ncg:
            global_scores(cg + 1)
    cs_mate.start()
    cn_mate.start()

    def merge_pair():
        cs_mate.wait_recv()
        cn_mate.wait_recv()
        a, b = cs_out[core].reshape(nc, LANES), cs_pair[...].reshape(nc, LANES)
        m = jnp.maximum(a, b)
        ea, eb = jnp.exp(a - m), jnp.exp(b - m)
        t = a * pltpu.roll(ea, hpb, 1) + b * pltpu.roll(eb, hpb, 1)
        cs_mid[...] = jnp.where(lane_f < hpb, m, t).reshape(nc, 1, LANES)
        clean = lane_f < hpb
        fa, fb = spread(jnp.where(clean, ea, 0.0)), spread(jnp.where(clean, eb, 0.0))
        for i in range(nc):
            rows = slice(i * rb, (i + 1) * rb)
            cn_mid[i] = (
                cn_out[core, i].astype(F32) * fa[rows] + cn_pair[i].astype(F32) * fb[rows]
            ).astype(BF)
        to_chips(lambda p: cs_mid.at[p], cs_in.at[chip], 2)
        to_chips(lambda p: cn_mid.at[p], cn_in.at[chip], 3)
        cs_in[chip] = cs_mid[chip]
        cn_in[chip] = cn_mid[chip]

    def choose(b):
        picks = []
        for r in range(RAND):
            rel = rb_ref[r, b] - me * nblk
            dev = lax.div(rel + FAR * nblk, nblk)
            slot = jnp.where(dev < FAR, dev, dev - 1)
            pick = jnp.where(dev == FAR, rel + 1, far0 + slot)
            picks.append(jnp.minimum(jnp.maximum(pick, 0), far0 + NFAR - 1))
        return picks

    def rows_of(which, p, b, picks):
        return jnp.concatenate(
            [kv[b + i, which, p] for i in range(3)]
            + [kv[i, which, p] for i in picks]
            + [kv[glob0 + i, which, p] for i in range(gblk)],
            axis=0,
        )

    half = pairs // 2
    nsub = (3 + RAND) * BLK // LANES + NG // LANES

    def wide(x):
        return jnp.concatenate([x] * nsub, axis=1)

    def scores(g, blk):
        t, b, picks, bias = blk
        for j in range(half):
            p = g * half + j
            s = lax.dot_general(
                stacked(kv[1 + b, 2, p]), rows_of(0, p, b, picks), NT, preferred_element_type=F32
            )
            if bias is not None:
                s = s + bias
            sc[g, j] = s
            top[g, j] = jnp.broadcast_to(
                jnp.max(s, axis=-1, keepdims=True), (2 * BLK, LANES)
            )

    def expo(g):
        for j in range(half):
            e = jnp.exp2((sc[g, j] - wide(top[g, j])) * EXP_SCALE)
            ex[g, j] = e
            inv[g, j] = jnp.broadcast_to(
                1.0 / jnp.sum(e, axis=-1, keepdims=True), (2 * BLK, LANES)
            )

    def weigh(g, blk):
        t, b, picks, _ = blk
        for j in range(0, half, 2):
            p = g * half + j
            w = jnp.concatenate(
                [(ex[g, j + i] * wide(inv[g, j + i])).astype(BF) for i in range(2)], axis=0
            )
            x = jnp.dot(
                w,
                jnp.concatenate([rows_of(1, p + i, b, picks) for i in range(2)], axis=1),
                preferred_element_type=F32,
            )
            for i in range(2):
                y = x[i * 2 * BLK:(i + 1) * 2 * BLK, i * LANES:(i + 1) * LANES]
                sp[t, p + i] = jnp.where(islo, y[:BLK], y[BLK:]).astype(BF)

    def attend(before, blocks):
        seq = [before] + blocks
        for i, blk in enumerate(blocks):
            expo(1)
            scores(0, blk)
            weigh(0, seq[i])
            expo(0)
            scores(1, blk)
            weigh(1, seq[i])

    def block_at(t, b, bias=None):
        return t, b, choose(b), bias

    def between():
        wait_chips(cs_in, all_r.at[2])
        wait_chips(cn_in, all_r.at[3])
        stat = cs_in[...].reshape(nc, LANES)
        e = jnp.exp(stat - jnp.max(stat, axis=0, keepdims=True))
        den = jnp.sum(pltpu.roll(stat, LANES - hpb, 1) * e, axis=0, keepdims=True)
        fac = spread(jnp.where(lane_f < hpb, e / den, 0.0))
        num = cn_in[0].astype(F32) * fac[0:rb]
        for i in range(1, nc):
            num = num + cn_in[i].astype(F32) * fac[i * rb:(i + 1) * rb]
        ag2[core, chip] = num.astype(BF)
        to_chips(lambda p: ag2.at[core, chip], ag2.at[core, chip], 4)

        for side, o in ((0, 1), (1, -1)):
            @pl.when(exists(o))
            def _():
                halo_copy(side).wait_recv()
        for i, o in enumerate(OFFSETS):
            @pl.when(exists(o))
            def _():
                far_copy(i).wait_recv()
        def project_edges(i, carry):
            rows = land[...].reshape((2 + NFAR) * BLK, width)
            val = jnp.dot(rows, wall[i], preferred_element_type=F32).astype(BF)
            for p in range(pairs):
                x = val[:, p * LANES:(p + 1) * LANES].reshape(2 + NFAR, BLK, LANES)
                kv[0, i, p] = x[0]
                kv[right0:glob0, i, p] = x[1:]
            return carry

        lax.fori_loop(0, 2, project_edges, 0)

    def two(i, carry):
        @pl.when(i == 1)
        def _():
            merge_pair()

        @pl.when(i == nblk // 4)
        def _():
            between()

        @pl.when(i == nblk // 4 + 2)
        def _():
            wait_chips(ag2.at[0], all_r.at[4])
            ag2_mate.start()

        prev = jnp.maximum(2 * i - 1, 0)
        attend(
            block_at(prev, order[prev]),
            [block_at(2 * i + j, order[2 * i + j]) for j in range(2)],
        )
        return carry

    lax.fori_loop(0, nblk // 2 - 1, two, 0)
    key_col = lax.broadcasted_iota(jnp.int32, (1, (3 + RAND) * BLK + NG), 1)
    lead = jnp.where(me == 0, BLK, 0)
    tail = jnp.where(me == n - 1, 2 * BLK, 3 * BLK)
    first = jnp.where(key_col < lead, -1e30, 0.0)
    last = jnp.where((key_col >= tail) & (key_col < 3 * BLK), -1e30, 0.0)
    end = block_at(nblk - 1, nblk - 1, last)
    attend(block_at(nblk - 3, order[nblk - 3]), [block_at(nblk - 2, 0, first), end])
    expo(1)
    weigh(0, end)
    weigh(1, end)

    ag2_mate.wait_recv()
    for d in range(n):
        r, c = (d // ncg) * rb, (d % ncg) * cb
        if rb % 16 == 0:
            gout[r:r + rb, c:c + cb] = ag2[d % 2, d // 2]
        else:
            gf[r:r + rb, c:c + cb] = ag2[d % 2, d // 2].astype(F32)
    if rb % 16:
        gout[...] = gf[...].astype(BF)

    for i, o in enumerate(OFFSETS):
        @pl.when(exists(o))
        def _():
            req_copy(i).wait_send()

        @pl.when(exists(-o))
        def _():
            far_copy(i).wait_send()
    for side, o in ((0, -1), (1, 1)):
        @pl.when(exists(o))
        def _():
            halo_copy(side).wait_send()
    for cp in (rs_mate, ag_mate, cs_mate, cn_mate, ag2_mate):
        cp.wait_send()
    for i, buf in enumerate((rs_mid, ag.at[0], cs_mid, cn_mid, ag2.at[0])):
        wait_chips(buf, all_s.at[i])


def mix(step, tok_dev, place, start_ref, sp, gout, grow_ref, wo, out_ref):
    c = pl.program_id(0)
    at = c * step
    pairs = sp.shape[1]
    pos = start_ref[0] + at + lax.broadcasted_iota(jnp.int32, (step, NG), 0)
    one = jnp.where(pos == grow_ref[...], 1.0, 0.0)
    is_g = jnp.max(one, axis=-1, keepdims=True) > 0.5
    put = jnp.dot(one.astype(BF), gout[...], preferred_element_type=F32)
    own = jnp.concatenate(
        [
            jnp.concatenate([sp[place[c * (step // BLK) + i], p] for p in range(pairs)], axis=1)
            for i in range(step // BLK)
        ],
        axis=0,
    )
    att = jnp.where(is_g, put, own.astype(F32)).astype(BF)
    out_ref[...] = jnp.dot(att, wo[...], preferred_element_type=F32).astype(BF)


def body(n, tokens, w_query, w_key, w_value, w_out, rand_blocks, global_pos):
    tok_dev, width = tokens.shape
    nblk = tok_dev // BLK
    pairs = width // LANES
    cb = 256 if n <= 32 else 128
    rb = NG * width // (n * cb)
    ext = nblk + 2 + NFAR + NG // BLK
    dma = pltpu.SemaphoreType.DMA
    vm = pltpu.VMEM
    nc = n // 2
    both = vm((2, nc, rb, cb), BF)
    piece = vm((nc, rb, cb), BF)
    stat = vm((nc, 1, LANES), F32)
    keys = (3 + RAND) * BLK + NG
    big = vm((2, pairs // 2, 2 * BLK, keys), F32)
    small = vm((2, pairs // 2, 2 * BLK, LANES), F32)
    scratch = [
        vm((nblk, BLK, width), BF), vm((3, width, width), BF),
        vm((ext, 3, pairs, BLK, LANES), BF),
        vm((NG, width), BF), vm((NG, width), F32), vm((NG, tok_dev), BF),
        vm((NFAR, BLK, width), BF), vm((2 + NFAR, BLK, width), BF),
        vm((NFAR, 8, LANES), jnp.int32), vm((NFAR, 8, LANES), jnp.int32),
        pltpu.SMEM((nblk,), jnp.int32),
        both, piece, piece, piece, both, both, piece, piece, piece,
        vm((2, nc, 1, LANES), F32), stat, stat, stat, both,
        big, small, big, small,
        vm((2, cb // LANES, 2 * NG, tok_dev), F32), vm((2, cb // LANES, 2 * NG, LANES), F32),
        dma((4,)), dma((NFAR,)), dma((NFAR,)), dma((2 + NFAR,)), dma((2 + NFAR,)),
        dma((5,)), dma((5,)), dma((5,)), dma((5,)),
    ]
    anyspace = pl.BlockSpec(memory_space=pl.ANY)
    vmem = pl.BlockSpec(memory_space=pltpu.VMEM)
    smem = pl.BlockSpec(memory_space=pltpu.SMEM)
    grow = global_pos.reshape(1, NG)
    rbt = rand_blocks.T
    sp, gout, place = pl.pallas_call(
        functools.partial(attention, n),
        out_shape=(
            jax.ShapeDtypeStruct((nblk, pairs, BLK, LANES), BF),
            jax.ShapeDtypeStruct((NG, width), BF),
            jax.ShapeDtypeStruct((nblk,), jnp.int32),
        ),
        in_specs=[anyspace] * 4 + [vmem] * 2 + [smem],
        out_specs=(vmem, vmem, smem),
        scratch_shapes=scratch,
        compiler_params=pltpu.CompilerParams(
            collective_id=0, has_side_effects=True, vmem_limit_bytes=51 << 20
        ),
        name="attention",
    )(tokens.reshape(nblk, BLK, width), w_query, w_key, w_value, rbt, grow, rbt)
    step = 256
    start = (lax.axis_index("seq") * tok_dev).reshape(1).astype(jnp.int32)
    return pl.pallas_call(
        functools.partial(mix, step, tok_dev),
        grid=(tok_dev // step,),
        out_shape=jax.ShapeDtypeStruct((tok_dev, width), BF),
        in_specs=[smem, smem, vmem, vmem, vmem, vmem],
        out_specs=pl.BlockSpec((step, width), lambda i: (i, 0)),
        compiler_params=pltpu.CompilerParams(vmem_limit_bytes=32 << 20),
        name="mix",
    )(place, start, sp, gout, grow, w_out)


def solution(mesh):
    placed = (P("seq", None), P(), P(), P(), P(), P("seq", None), P())
    return jax.shard_map(
        functools.partial(body, mesh.shape["seq"]), mesh=mesh, in_specs=placed,
        out_specs=P("seq", None), check_vma=False,
    )
```

```python
import functools
import math

import jax
import jax.numpy as jnp
from jax import lax
from jax.experimental import pallas as pl
from jax.experimental.pallas import tpu as pltpu
from jax.sharding import PartitionSpec as P

HEADS = 16
HD = 64
BLK = 64
RAND = 3
NG = 128
FAR = 3
OFFSETS = tuple(range(-FAR, 0)) + tuple(range(1, FAR + 1))
NFAR = len(OFFSETS)
LANES = 128
EXP_SCALE = math.log2(math.e) / math.sqrt(HD)
SCORE_SCALE = 1.0 / math.sqrt(HD)
MESH = pl.DeviceIdType.MESH
BF = jnp.bfloat16
F32 = jnp.float32
NT = (((1,), (1,)), ((), ()))


def attention(
    n,
    tok_hbm, wq_hbm, wk_hbm, wv_hbm, rbv_ref, grow_ref, rb_ref,
    sp, gout, place,
    xt, wall, kv, xg, gf, sel, far, land,
    req_out, reqin, order,
    rs_out, rs_pair, rs_mid, rs_in, ag, cn_out, cn_pair, cn_mid, cn_in,
    cs_out, cs_pair, cs_mid, cs_in, ag2,
    sc, top, ex, inv, gsc, gtop,
    load_sem, req_s, req_r, edge_s, edge_r, one_s, one_r, all_s, all_r,
):
    nblk, _, width = tok_hbm.shape
    tok_dev = nblk * BLK
    me = lax.axis_index("seq")
    core, chip = lax.rem(me, 2), lax.div(me, 2)
    mate = me + 1 - 2 * core
    _, nc, rb, cb = ag.shape
    ncg = width // cb
    hpb = cb // HD
    pairs = width // LANES
    right0 = nblk + 1
    far0 = nblk + 2
    glob0 = far0 + NFAR
    gblk = NG // BLK

    loads = [
        pltpu.make_async_copy(src, dst, load_sem.at[i])
        for i, (src, dst) in enumerate(
            (
                (tok_hbm, xt), (wk_hbm, wall.at[0]), (wv_hbm, wall.at[1]),
                (wq_hbm, wall.at[2]),
            )
        )
    ]
    for cp in loads:
        cp.start()

    land[...] = jnp.zeros(land.shape, BF)
    reqin[...] = jnp.zeros(reqin.shape, jnp.int32)
    base = rbv_ref[RAND - 1:RAND, :] - me * nblk
    for i, o in enumerate(OFFSETS):
        loc = base - o * nblk
        loc = jnp.where((loc >= 0) & (loc < nblk), loc, 0)
        want = jnp.sum(loc, axis=1, keepdims=True)
        req_out[i] = jnp.broadcast_to(want, (8, LANES))

    def exists(o):
        return me + o >= 0 if o < 0 else me + o < n

    barrier = pltpu.get_barrier_semaphore()
    other = me - 1 + 2 * core

    def greet(device):
        pl.semaphore_signal(barrier, inc=1, device_id=(device,), device_id_type=MESH)

    def greet_chip(o, c):
        greet(2 * lax.rem(chip + o, nc) + core)
        return c

    lax.fori_loop(1, nc, greet_chip, 0)
    greet(mate)
    there = ((other >= 0) & (other < n), other), (exists(-FAR), me - FAR), (exists(FAR), me + FAR)
    for ok, device in there:
        @pl.when(ok)
        def _():
            greet(device)

    def to_chips(src, dst, i):
        def one(o, c):
            peer = lax.rem(chip + o, nc)
            pltpu.make_async_remote_copy(
                src_ref=src(peer), dst_ref=dst, send_sem=all_s.at[i], recv_sem=all_r.at[i],
                device_id=(2 * peer + core,), device_id_type=MESH,
            ).start()
            return c

        lax.fori_loop(1, nc, one, 0)

    def wait_chips(buf, sem):
        part = buf.at[pl.ds(0, nc - 1)]
        pltpu.make_async_copy(part, part, sem).wait()

    def to_mate(src, dst, i):
        return pltpu.make_async_remote_copy(
            src_ref=src, dst_ref=dst, send_sem=one_s.at[i], recv_sem=one_r.at[i],
            device_id=(mate,), device_id_type=MESH,
        )

    rs_mate = to_mate(rs_out.at[1 - core], rs_pair, 0)
    ag_mate = to_mate(ag.at[core], ag.at[core], 1)
    cs_mate = to_mate(cs_out.at[1 - core], cs_pair, 2)
    cn_mate = to_mate(cn_out.at[1 - core], cn_pair, 3)
    ag2_mate = to_mate(ag2.at[core], ag2.at[core], 4)

    def req_copy(i):
        return pltpu.make_async_remote_copy(
            src_ref=req_out.at[i], dst_ref=reqin.at[i], send_sem=req_s.at[i],
            recv_sem=req_r.at[i], device_id=(me + OFFSETS[i],), device_id_type=MESH,
        )

    def far_copy(i):
        return pltpu.make_async_remote_copy(
            src_ref=far.at[i],
            dst_ref=land.at[2 + i],
            send_sem=edge_s.at[2 + i], recv_sem=edge_r.at[2 + i],
            device_id=(me - OFFSETS[i],), device_id_type=MESH,
        )

    def halo_copy(side):
        src, dst, dev = (0, 1, me - 1) if side == 0 else (nblk - 1, 0, me + 1)
        return pltpu.make_async_remote_copy(
            src_ref=xt.at[src], dst_ref=land.at[dst],
            send_sem=edge_s.at[side], recv_sem=edge_r.at[side],
            device_id=(dev,), device_id_type=MESH,
        )

    diag = lax.broadcasted_iota(jnp.int32, (NG, NG), 0) == lax.broadcasted_iota(
        jnp.int32, (NG, NG), 1
    )
    gcol = jnp.sum(
        jnp.where(diag, (grow_ref[...] - me * tok_dev).astype(F32), 0.0), axis=1, keepdims=True
    )
    hit = gcol == lax.broadcasted_iota(jnp.int32, (NG, tok_dev), 1).astype(F32)
    sel[...] = jnp.where(hit, 1.0, 0.0).astype(BF)

    loads[0].wait()
    picked = jnp.dot(sel[...], xt[...].reshape(tok_dev, width), preferred_element_type=F32)
    if rb % 16 == 0:
        picked = picked.astype(BF)
        for d in range(n):
            r, c = (d // ncg) * rb, (d % ncg) * cb
            rs_out[d % 2, d // 2] = picked[r:r + rb, c:c + cb]
    else:
        gf[...] = picked
        for d in range(n):
            r, c = (d // ncg) * rb, (d % ncg) * cb
            rs_out[d % 2, d // 2] = gf[r:r + rb, c:c + cb].astype(BF)
    pl.semaphore_wait(barrier, nc + sum(jnp.where(ok, 1, 0) for ok, _ in there))
    rs_mate.start()
    for i, o in enumerate(OFFSETS):
        @pl.when(exists(o))
        def _():
            req_copy(i).start()


    def reduce_pair():
        rs_mate.wait_recv()
        rs_mid[...] = rs_out[core] + rs_pair[...]
        to_chips(lambda p: rs_mid.at[p], rs_in.at[chip], 0)
        rs_in[chip] = rs_mid[chip]

    def gather():
        wait_chips(rs_in, all_r.at[0])
        ag[core, chip] = jnp.sum(rs_in[...].astype(F32), axis=0).astype(BF)
        to_chips(lambda p: ag.at[core, chip], ag.at[core, chip], 1)

    def send_edges():
        for side, o in ((0, -1), (1, 1)):
            @pl.when(exists(o))
            def _():
                halo_copy(side).start()
        for i, o in enumerate(OFFSETS):
            @pl.when(exists(-o))
            def _():
                req_copy(i).wait_recv()
        for i, o in enumerate(OFFSETS):
            want = jnp.minimum(jnp.maximum(reqin[i, 0, 0], 0), nblk - 1)
            far[i] = xt[want]

            @pl.when(exists(-o))
            def _():
                far_copy(i).start()

    def gather_pair():
        wait_chips(ag.at[0], all_r.at[1])
        ag_mate.start()

    step = 512
    parts = tok_dev // step

    def project(c, carry):
        for i in range(3):
            @pl.when(c == i * parts)
            def _():
                loads[1 + i].wait()

        for at, act in ((1, reduce_pair), (3, gather), (3, send_edges), (5, gather_pair)):
            @pl.when(c == at)
            def _():
                act()

        which, part = lax.div(c, parts), lax.rem(c, parts)
        rows = xt[pl.ds(part * (step // BLK), step // BLK)].reshape(step, width)
        val = jnp.dot(rows, wall[which], preferred_element_type=F32).astype(BF)
        for p in range(pairs):
            kv[pl.ds(1 + part * (step // BLK), step // BLK), which, p] = val[
                :, p * LANES:(p + 1) * LANES
            ].reshape(step // BLK, BLK, LANES)
        return carry

    lax.fori_loop(0, 3 * parts, project, 0)

    lates = []
    for b in range(1, nblk - 1):
        r = rb_ref[RAND - 1, b] - me * nblk
        lates.append(jnp.where((r >= 0) & (r < nblk), 0, 1))
    early = nblk - 2 - sum(lates)
    seen = jnp.int32(0)
    spots = []
    for b in range(1, nblk - 1):
        late = lates[b - 1]
        spots.append(jnp.where(late == 1, early + seen, b - 1 - seen))
        seen = seen + late
        place[b] = spots[b - 1]
    for t in range(nblk - 2):
        order[t] = sum(jnp.where(spots[b - 1] == t, b, 0) for b in range(1, nblk - 1))
    place[0] = nblk - 2
    place[nblk - 1] = nblk - 1

    ag_mate.wait_recv()
    for d in range(n):
        r, c = (d // ncg) * rb, (d % ncg) * cb
        if rb % 16 == 0:
            xg[r:r + rb, c:c + cb] = ag[d % 2, d // 2]
        else:
            gf[r:r + rb, c:c + cb] = ag[d % 2, d // 2].astype(F32)
    if rb % 16:
        xg[...] = gf[...].astype(BF)

    def project_global(i, carry):
        val = jnp.dot(xg[...], wall[i], preferred_element_type=F32).astype(BF)
        for p in range(pairs):
            kv[glob0:glob0 + gblk, i, p] = val[:, p * LANES:(p + 1) * LANES].reshape(
                gblk, BLK, LANES
            )
        return carry

    lax.fori_loop(0, 3, project_global, 0)

    lane = lax.broadcasted_iota(jnp.int32, (1, LANES), 1)
    islo = lane < HD
    halves = (jnp.where(islo, 1.0, 0.0).astype(BF), jnp.where(islo, 0.0, 1.0).astype(BF))
    wide_row = LANES // rb
    lane_f = jnp.bitwise_and(lane, wide_row - 1)
    own_row = lax.shift_right_logical(
        lax.broadcasted_iota(jnp.int32, (rb, LANES), 1), wide_row.bit_length() - 1
    ) == lax.broadcasted_iota(jnp.int32, (rb, LANES), 0)
    head_of = jnp.where(
        jnp.bitwise_and(lax.broadcasted_iota(jnp.int32, (LANES, cb), 0), wide_row - 1)
        == lax.shift_right_logical(lax.broadcasted_iota(jnp.int32, (LANES, cb), 1), 6),
        1.0, 0.0,
    )

    def flat(x):
        return jnp.sum(jnp.where(own_row, x, 0.0), axis=0, keepdims=True)

    def spread(x):
        rows = [jnp.where(own_row, x[i:i + 1], 0.0) for i in range(nc)]
        return jnp.dot(
            jnp.concatenate(rows, axis=0), head_of, preferred_element_type=F32,
            precision=lax.Precision.HIGHEST,
        )

    def stacked(x):
        return jnp.concatenate([x * m for m in halves], axis=0)

    def with_ones(x):
        return jnp.concatenate([x, jnp.ones(x.shape, BF)], axis=1)

    per = cb // LANES

    def global_scores(cg):
        for j in range(per):
            p = cg * per + j
            s = lax.dot_general(
                stacked(kv[glob0:glob0 + gblk, 2, p].reshape(NG, LANES)),
                kv[1:1 + nblk, 0, p].reshape(tok_dev, LANES), NT,
                preferred_element_type=F32,
            )
            gsc[cg % 2, j] = s
            gtop[cg % 2, j] = jnp.broadcast_to(
                jnp.max(s, axis=-1, keepdims=True), (2 * NG, LANES)
            )

    def global_sums(cg):
        nums, stat = [], jnp.zeros((NG, LANES), F32)
        for j in range(per):
            p = cg * per + j
            m = gtop[cg % 2, j]
            shift = jnp.concatenate([m] * (tok_dev // LANES), axis=1)
            e = jnp.exp2((gsc[cg % 2, j] - shift) * EXP_SCALE).astype(BF)
            x = jnp.dot(
                e, with_ones(kv[1:1 + nblk, 1, p].reshape(tok_dev, LANES)),
                preferred_element_type=F32,
            )
            nums.append(jnp.where(islo, x[:NG, :LANES], x[NG:, :LANES]).astype(BF))
            m = m * SCORE_SCALE
            for h in range(2):
                rows = slice(h * NG, (h + 1) * NG)
                stat = jnp.where(lane_f == 2 * j + h, m[rows], stat)
                stat = jnp.where(lane_f == hpb + 2 * j + h, x[rows, LANES:], stat)
        num = jnp.concatenate(nums, axis=1) if per > 1 else nums[0]
        for rg in range(NG // rb):
            d = rg * ncg + cg
            cn_out[d % 2, d // 2] = num[rg * rb:(rg + 1) * rb]
            cs_out[d % 2, d // 2] = flat(stat[rg * rb:(rg + 1) * rb])

    global_scores(0)
    for cg in range(ncg):
        global_sums(cg)
        if cg + 1 < ncg:
            global_scores(cg + 1)
    cs_mate.start()
    cn_mate.start()

    def merge_pair():
        cs_mate.wait_recv()
        cn_mate.wait_recv()
        a, b = cs_out[core].reshape(nc, LANES), cs_pair[...].reshape(nc, LANES)
        m = jnp.maximum(a, b)
        ea, eb = jnp.exp(a - m), jnp.exp(b - m)
        t = a * pltpu.roll(ea, hpb, 1) + b * pltpu.roll(eb, hpb, 1)
        cs_mid[...] = jnp.where(lane_f < hpb, m, t).reshape(nc, 1, LANES)
        clean = lane_f < hpb
        fa, fb = spread(jnp.where(clean, ea, 0.0)), spread(jnp.where(clean, eb, 0.0))
        for i in range(nc):
            rows = slice(i * rb, (i + 1) * rb)
            cn_mid[i] = (
                cn_out[core, i].astype(F32) * fa[rows] + cn_pair[i].astype(F32) * fb[rows]
            ).astype(BF)
        to_chips(lambda p: cs_mid.at[p], cs_in.at[chip], 2)
        to_chips(lambda p: cn_mid.at[p], cn_in.at[chip], 3)
        cs_in[chip] = cs_mid[chip]
        cn_in[chip] = cn_mid[chip]

    def choose(b):
        picks = []
        for r in range(RAND):
            rel = rb_ref[r, b] - me * nblk
            dev = lax.div(rel + FAR * nblk, nblk)
            slot = jnp.where(dev < FAR, dev, dev - 1)
            pick = jnp.where(dev == FAR, rel + 1, far0 + slot)
            picks.append(jnp.minimum(jnp.maximum(pick, 0), far0 + NFAR - 1))
        return picks

    def rows_of(which, p, b, picks):
        return jnp.concatenate(
            [kv[b + i, which, p] for i in range(3)]
            + [kv[i, which, p] for i in picks]
            + [kv[glob0 + i, which, p] for i in range(gblk)],
            axis=0,
        )

    half = pairs // 2
    nsub = (3 + RAND) * BLK // LANES + NG // LANES

    def wide(x):
        return jnp.concatenate([x] * nsub, axis=1)

    def scores(g, blk):
        t, b, picks, bias = blk
        for j in range(half):
            p = g * half + j
            s = lax.dot_general(
                stacked(kv[1 + b, 2, p]), rows_of(0, p, b, picks), NT, preferred_element_type=F32
            )
            if bias is not None:
                s = s + bias
            sc[g, j] = s
            top[g, j] = jnp.broadcast_to(
                jnp.max(s, axis=-1, keepdims=True), (2 * BLK, LANES)
            )

    def expo(g):
        for j in range(half):
            e = jnp.exp2((sc[g, j] - wide(top[g, j])) * EXP_SCALE)
            ex[g, j] = e
            inv[g, j] = jnp.broadcast_to(
                1.0 / jnp.sum(e, axis=-1, keepdims=True), (2 * BLK, LANES)
            )

    def weigh(g, blk):
        t, b, picks, _ = blk
        for j in range(0, half, 2):
            p = g * half + j
            w = jnp.concatenate(
                [(ex[g, j + i] * wide(inv[g, j + i])).astype(BF) for i in range(2)], axis=0
            )
            x = jnp.dot(
                w,
                jnp.concatenate([rows_of(1, p + i, b, picks) for i in range(2)], axis=1),
                preferred_element_type=F32,
            )
            for i in range(2):
                y = x[i * 2 * BLK:(i + 1) * 2 * BLK, i * LANES:(i + 1) * LANES]
                sp[t, p + i] = jnp.where(islo, y[:BLK], y[BLK:]).astype(BF)

    def attend(before, blocks):
        seq = [before] + blocks
        for i, blk in enumerate(blocks):
            expo(1)
            scores(0, blk)
            weigh(0, seq[i])
            expo(0)
            scores(1, blk)
            weigh(1, seq[i])

    def block_at(t, b, bias=None):
        return t, b, choose(b), bias

    def between():
        wait_chips(cs_in, all_r.at[2])
        wait_chips(cn_in, all_r.at[3])
        stat = cs_in[...].reshape(nc, LANES)
        e = jnp.exp(stat - jnp.max(stat, axis=0, keepdims=True))
        den = jnp.sum(pltpu.roll(stat, LANES - hpb, 1) * e, axis=0, keepdims=True)
        fac = spread(jnp.where(lane_f < hpb, e / den, 0.0))
        num = cn_in[0].astype(F32) * fac[0:rb]
        for i in range(1, nc):
            num = num + cn_in[i].astype(F32) * fac[i * rb:(i + 1) * rb]
        ag2[core, chip] = num.astype(BF)
        to_chips(lambda p: ag2.at[core, chip], ag2.at[core, chip], 4)

        for side, o in ((0, 1), (1, -1)):
            @pl.when(exists(o))
            def _():
                halo_copy(side).wait_recv()
        for i, o in enumerate(OFFSETS):
            @pl.when(exists(o))
            def _():
                far_copy(i).wait_recv()
        def project_edges(i, carry):
            rows = land[...].reshape((2 + NFAR) * BLK, width)
            val = jnp.dot(rows, wall[i], preferred_element_type=F32).astype(BF)
            for p in range(pairs):
                x = val[:, p * LANES:(p + 1) * LANES].reshape(2 + NFAR, BLK, LANES)
                kv[0, i, p] = x[0]
                kv[right0:glob0, i, p] = x[1:]
            return carry

        lax.fori_loop(0, 2, project_edges, 0)

    def two(i, carry):
        @pl.when(i == 1)
        def _():
            merge_pair()

        @pl.when(i == nblk // 4)
        def _():
            between()

        prev = jnp.maximum(2 * i - 1, 0)
        attend(
            block_at(prev, order[prev]),
            [block_at(2 * i + j, order[2 * i + j]) for j in range(2)],
        )
        return carry

    lax.fori_loop(0, nblk // 2 - 1, two, 0)
    wait_chips(ag2.at[0], all_r.at[4])
    ag2_mate.start()
    key_col = lax.broadcasted_iota(jnp.int32, (1, (3 + RAND) * BLK + NG), 1)
    lead = jnp.where(me == 0, BLK, 0)
    tail = jnp.where(me == n - 1, 2 * BLK, 3 * BLK)
    first = jnp.where(key_col < lead, -1e30, 0.0)
    last = jnp.where((key_col >= tail) & (key_col < 3 * BLK), -1e30, 0.0)
    end = block_at(nblk - 1, nblk - 1, last)
    attend(block_at(nblk - 3, order[nblk - 3]), [block_at(nblk - 2, 0, first), end])
    expo(1)
    weigh(0, end)
    weigh(1, end)

    ag2_mate.wait_recv()
    for d in range(n):
        r, c = (d // ncg) * rb, (d % ncg) * cb
        if rb % 16 == 0:
            gout[r:r + rb, c:c + cb] = ag2[d % 2, d // 2]
        else:
            gf[r:r + rb, c:c + cb] = ag2[d % 2, d // 2].astype(F32)
    if rb % 16:
        gout[...] = gf[...].astype(BF)

    for i, o in enumerate(OFFSETS):
        @pl.when(exists(o))
        def _():
            req_copy(i).wait_send()

        @pl.when(exists(-o))
        def _():
            far_copy(i).wait_send()
    for side, o in ((0, -1), (1, 1)):
        @pl.when(exists(o))
        def _():
            halo_copy(side).wait_send()
    for cp in (rs_mate, ag_mate, cs_mate, cn_mate, ag2_mate):
        cp.wait_send()
    for i, buf in enumerate((rs_mid, ag.at[0], cs_mid, cn_mid, ag2.at[0])):
        wait_chips(buf, all_s.at[i])


def mix(step, tok_dev, place, start_ref, sp, gout, grow_ref, wo, out_ref):
    c = pl.program_id(0)
    at = c * step
    pairs = sp.shape[1]
    pos = start_ref[0] + at + lax.broadcasted_iota(jnp.int32, (step, NG), 0)
    one = jnp.where(pos == grow_ref[...], 1.0, 0.0)
    is_g = jnp.max(one, axis=-1, keepdims=True) > 0.5
    put = jnp.dot(one.astype(BF), gout[...], preferred_element_type=F32)
    own = jnp.concatenate(
        [
            jnp.concatenate([sp[place[c * (step // BLK) + i], p] for p in range(pairs)], axis=1)
            for i in range(step // BLK)
        ],
        axis=0,
    )
    att = jnp.where(is_g, put, own.astype(F32)).astype(BF)
    out_ref[...] = jnp.dot(att, wo[...], preferred_element_type=F32).astype(BF)


def body(n, tokens, w_query, w_key, w_value, w_out, rand_blocks, global_pos):
    tok_dev, width = tokens.shape
    nblk = tok_dev // BLK
    pairs = width // LANES
    cb = 256 if n <= 32 else 128
    rb = NG * width // (n * cb)
    ext = nblk + 2 + NFAR + NG // BLK
    dma = pltpu.SemaphoreType.DMA
    vm = pltpu.VMEM
    nc = n // 2
    both = vm((2, nc, rb, cb), BF)
    piece = vm((nc, rb, cb), BF)
    stat = vm((nc, 1, LANES), F32)
    keys = (3 + RAND) * BLK + NG
    big = vm((2, pairs // 2, 2 * BLK, keys), F32)
    small = vm((2, pairs // 2, 2 * BLK, LANES), F32)
    scratch = [
        vm((nblk, BLK, width), BF), vm((3, width, width), BF),
        vm((ext, 3, pairs, BLK, LANES), BF),
        vm((NG, width), BF), vm((NG, width), F32), vm((NG, tok_dev), BF),
        vm((NFAR, BLK, width), BF), vm((2 + NFAR, BLK, width), BF),
        vm((NFAR, 8, LANES), jnp.int32), vm((NFAR, 8, LANES), jnp.int32),
        pltpu.SMEM((nblk,), jnp.int32),
        both, piece, piece, piece, both, both, piece, piece, piece,
        vm((2, nc, 1, LANES), F32), stat, stat, stat, both,
        big, small, big, small,
        vm((2, cb // LANES, 2 * NG, tok_dev), F32), vm((2, cb // LANES, 2 * NG, LANES), F32),
        dma((4,)), dma((NFAR,)), dma((NFAR,)), dma((2 + NFAR,)), dma((2 + NFAR,)),
        dma((5,)), dma((5,)), dma((5,)), dma((5,)),
    ]
    anyspace = pl.BlockSpec(memory_space=pl.ANY)
    vmem = pl.BlockSpec(memory_space=pltpu.VMEM)
    smem = pl.BlockSpec(memory_space=pltpu.SMEM)
    grow = global_pos.reshape(1, NG)
    rbt = rand_blocks.T
    sp, gout, place = pl.pallas_call(
        functools.partial(attention, n),
        out_shape=(
            jax.ShapeDtypeStruct((nblk, pairs, BLK, LANES), BF),
            jax.ShapeDtypeStruct((NG, width), BF),
            jax.ShapeDtypeStruct((nblk,), jnp.int32),
        ),
        in_specs=[anyspace] * 4 + [vmem] * 2 + [smem],
        out_specs=(vmem, vmem, smem),
        scratch_shapes=scratch,
        compiler_params=pltpu.CompilerParams(
            collective_id=0, has_side_effects=True, vmem_limit_bytes=51 << 20
        ),
        name="attention",
    )(tokens.reshape(nblk, BLK, width), w_query, w_key, w_value, rbt, grow, rbt)
    step = 512
    start = (lax.axis_index("seq") * tok_dev).reshape(1).astype(jnp.int32)
    return pl.pallas_call(
        functools.partial(mix, step, tok_dev),
        grid=(tok_dev // step,),
        out_shape=jax.ShapeDtypeStruct((tok_dev, width), BF),
        in_specs=[smem, smem, vmem, vmem, vmem, vmem],
        out_specs=pl.BlockSpec((step, width), lambda i: (i, 0)),
        compiler_params=pltpu.CompilerParams(vmem_limit_bytes=32 << 20),
        name="mix",
    )(place, start, sp, gout, grow, w_out)


def solution(mesh):
    placed = (P("seq", None), P(), P(), P(), P(), P("seq", None), P())
    return jax.shard_map(
        functools.partial(body, mesh.shape["seq"]), mesh=mesh, in_specs=placed,
        out_specs=P("seq", None), check_vma=False,
    )
```

```python
import functools
import math

import jax
import jax.numpy as jnp
from jax import lax
from jax.experimental import pallas as pl
from jax.experimental.pallas import tpu as pltpu
from jax.sharding import PartitionSpec as P

HEADS = 16
HD = 64
BLK = 64
RAND = 3
NG = 128
FAR = 3
OFFSETS = tuple(range(-FAR, 0)) + tuple(range(1, FAR + 1))
NFAR = len(OFFSETS)
LANES = 128
EXP_SCALE = math.log2(math.e) / math.sqrt(HD)
SCORE_SCALE = 1.0 / math.sqrt(HD)
MESH = pl.DeviceIdType.MESH
BF = jnp.bfloat16
F32 = jnp.float32
NT = (((1,), (1,)), ((), ()))


def attention(
    n,
    tok_hbm, wq_hbm, wk_hbm, wv_hbm, rbv_ref, grow_ref, rb_ref,
    sp, gout, place,
    xt, wall, kv, xg, gf, sel, far, land,
    req_out, reqin, order,
    rs_out, rs_pair, rs_mid, rs_in, ag, cn_out, cn_pair, cn_mid, cn_in,
    cs_out, cs_pair, cs_mid, cs_in, ag2,
    sc, top, ex, inv, gsc, gtop,
    load_sem, req_s, req_r, edge_s, edge_r, one_s, one_r, all_s, all_r,
):
    nblk, _, width = tok_hbm.shape
    tok_dev = nblk * BLK
    me = lax.axis_index("seq")
    core, chip = lax.rem(me, 2), lax.div(me, 2)
    mate = me + 1 - 2 * core
    _, nc, rb, cb = ag.shape
    ncg = width // cb
    hpb = cb // HD
    pairs = width // LANES
    right0 = nblk + 1
    far0 = nblk + 2
    glob0 = far0 + NFAR
    gblk = NG // BLK

    loads = [
        pltpu.make_async_copy(src, dst, load_sem.at[i])
        for i, (src, dst) in enumerate(
            (
                (tok_hbm, xt), (wk_hbm, wall.at[0]), (wv_hbm, wall.at[1]),
                (wq_hbm, wall.at[2]),
            )
        )
    ]
    for cp in loads:
        cp.start()

    land[...] = jnp.zeros(land.shape, BF)
    reqin[...] = jnp.zeros(reqin.shape, jnp.int32)
    base = rbv_ref[RAND - 1:RAND, :] - me * nblk
    for i, o in enumerate(OFFSETS):
        loc = base - o * nblk
        loc = jnp.where((loc >= 0) & (loc < nblk), loc, 0)
        want = jnp.sum(loc, axis=1, keepdims=True)
        req_out[i] = jnp.broadcast_to(want, (8, LANES))

    def exists(o):
        return me + o >= 0 if o < 0 else me + o < n

    barrier = pltpu.get_barrier_semaphore()
    other = me - 1 + 2 * core

    def greet(device):
        pl.semaphore_signal(barrier, inc=1, device_id=(device,), device_id_type=MESH)

    def greet_chip(o, c):
        greet(2 * lax.rem(chip + o, nc) + core)
        return c

    lax.fori_loop(1, nc, greet_chip, 0)
    greet(mate)
    there = ((other >= 0) & (other < n), other), (exists(-FAR), me - FAR), (exists(FAR), me + FAR)
    for ok, device in there:
        @pl.when(ok)
        def _():
            greet(device)

    def to_chips(src, dst, i):
        def one(o, c):
            peer = lax.rem(chip + o, nc)
            pltpu.make_async_remote_copy(
                src_ref=src(peer), dst_ref=dst, send_sem=all_s.at[i], recv_sem=all_r.at[i],
                device_id=(2 * peer + core,), device_id_type=MESH,
            ).start()
            return c

        lax.fori_loop(1, nc, one, 0)

    def wait_chips(buf, sem):
        part = buf.at[pl.ds(0, nc - 1)]
        pltpu.make_async_copy(part, part, sem).wait()

    def to_mate(src, dst, i):
        return pltpu.make_async_remote_copy(
            src_ref=src, dst_ref=dst, send_sem=one_s.at[i], recv_sem=one_r.at[i],
            device_id=(mate,), device_id_type=MESH,
        )

    rs_mate = to_mate(rs_out.at[1 - core], rs_pair, 0)
    ag_mate = to_mate(ag.at[core], ag.at[core], 1)
    cs_mate = to_mate(cs_out.at[1 - core], cs_pair, 2)
    cn_mate = to_mate(cn_out.at[1 - core], cn_pair, 3)
    ag2_mate = to_mate(ag2.at[core], ag2.at[core], 4)

    def req_copy(i):
        return pltpu.make_async_remote_copy(
            src_ref=req_out.at[i], dst_ref=reqin.at[i], send_sem=req_s.at[i],
            recv_sem=req_r.at[i], device_id=(me + OFFSETS[i],), device_id_type=MESH,
        )

    def far_copy(i):
        return pltpu.make_async_remote_copy(
            src_ref=far.at[i],
            dst_ref=land.at[2 + i],
            send_sem=edge_s.at[2 + i], recv_sem=edge_r.at[2 + i],
            device_id=(me - OFFSETS[i],), device_id_type=MESH,
        )

    def halo_copy(side):
        src, dst, dev = (0, 1, me - 1) if side == 0 else (nblk - 1, 0, me + 1)
        return pltpu.make_async_remote_copy(
            src_ref=xt.at[src], dst_ref=land.at[dst],
            send_sem=edge_s.at[side], recv_sem=edge_r.at[side],
            device_id=(dev,), device_id_type=MESH,
        )

    diag = lax.broadcasted_iota(jnp.int32, (NG, NG), 0) == lax.broadcasted_iota(
        jnp.int32, (NG, NG), 1
    )
    gcol = jnp.sum(
        jnp.where(diag, (grow_ref[...] - me * tok_dev).astype(F32), 0.0), axis=1, keepdims=True
    )
    hit = gcol == lax.broadcasted_iota(jnp.int32, (NG, tok_dev), 1).astype(F32)
    sel[...] = jnp.where(hit, 1.0, 0.0).astype(BF)

    loads[0].wait()
    picked = jnp.dot(sel[...], xt[...].reshape(tok_dev, width), preferred_element_type=F32)
    if rb % 16 == 0:
        picked = picked.astype(BF)
        for d in range(n):
            r, c = (d // ncg) * rb, (d % ncg) * cb
            rs_out[d % 2, d // 2] = picked[r:r + rb, c:c + cb]
    else:
        gf[...] = picked
        for d in range(n):
            r, c = (d // ncg) * rb, (d % ncg) * cb
            rs_out[d % 2, d // 2] = gf[r:r + rb, c:c + cb].astype(BF)
    pl.semaphore_wait(barrier, nc + sum(jnp.where(ok, 1, 0) for ok, _ in there))
    rs_mate.start()
    for i, o in enumerate(OFFSETS):
        @pl.when(exists(o))
        def _():
            req_copy(i).start()


    def reduce_pair():
        rs_mate.wait_recv()
        rs_mid[...] = rs_out[core] + rs_pair[...]
        to_chips(lambda p: rs_mid.at[p], rs_in.at[chip], 0)
        rs_in[chip] = rs_mid[chip]

    def gather():
        wait_chips(rs_in, all_r.at[0])
        ag[core, chip] = jnp.sum(rs_in[...].astype(F32), axis=0).astype(BF)
        to_chips(lambda p: ag.at[core, chip], ag.at[core, chip], 1)

    def send_edges():
        for side, o in ((0, -1), (1, 1)):
            @pl.when(exists(o))
            def _():
                halo_copy(side).start()
        for i, o in enumerate(OFFSETS):
            @pl.when(exists(-o))
            def _():
                req_copy(i).wait_recv()
        for i, o in enumerate(OFFSETS):
            want = jnp.minimum(jnp.maximum(reqin[i, 0, 0], 0), nblk - 1)
            far[i] = xt[want]

            @pl.when(exists(-o))
            def _():
                far_copy(i).start()

    def gather_pair():
        wait_chips(ag.at[0], all_r.at[1])
        ag_mate.start()

    step = 512
    parts = tok_dev // step

    def project(c, carry):
        for i in range(3):
            @pl.when(c == i * parts)
            def _():
                loads[1 + i].wait()

        for at, act in ((1, reduce_pair), (3, gather), (3, send_edges), (5, gather_pair)):
            @pl.when(c == at)
            def _():
                act()

        which, part = lax.div(c, parts), lax.rem(c, parts)
        rows = xt[pl.ds(part * (step // BLK), step // BLK)].reshape(step, width)
        val = jnp.dot(rows, wall[which], preferred_element_type=F32).astype(BF)
        for p in range(pairs):
            kv[pl.ds(1 + part * (step // BLK), step // BLK), which, p] = val[
                :, p * LANES:(p + 1) * LANES
            ].reshape(step // BLK, BLK, LANES)
        return carry

    lax.fori_loop(0, 3 * parts, project, 0)

    lates = []
    for b in range(1, nblk - 1):
        r = rb_ref[RAND - 1, b] - me * nblk
        lates.append(jnp.where((r >= 0) & (r < nblk), 0, 1))
    early = nblk - 2 - sum(lates)
    seen = jnp.int32(0)
    spots = []
    for b in range(1, nblk - 1):
        late = lates[b - 1]
        spots.append(jnp.where(late == 1, early + seen, b - 1 - seen))
        seen = seen + late
        place[b] = spots[b - 1]
    for t in range(nblk - 2):
        order[t] = sum(jnp.where(spots[b - 1] == t, b, 0) for b in range(1, nblk - 1))
    place[0] = nblk - 2
    place[nblk - 1] = nblk - 1

    ag_mate.wait_recv()
    for d in range(n):
        r, c = (d // ncg) * rb, (d % ncg) * cb
        if rb % 16 == 0:
            xg[r:r + rb, c:c + cb] = ag[d % 2, d // 2]
        else:
            gf[r:r + rb, c:c + cb] = ag[d % 2, d // 2].astype(F32)
    if rb % 16:
        xg[...] = gf[...].astype(BF)

    def project_global(i, carry):
        val = jnp.dot(xg[...], wall[i], preferred_element_type=F32).astype(BF)
        for p in range(pairs):
            kv[glob0:glob0 + gblk, i, p] = val[:, p * LANES:(p + 1) * LANES].reshape(
                gblk, BLK, LANES
            )
        return carry

    lax.fori_loop(0, 3, project_global, 0)

    lane = lax.broadcasted_iota(jnp.int32, (1, LANES), 1)
    islo = lane < HD
    halves = (jnp.where(islo, 1.0, 0.0).astype(BF), jnp.where(islo, 0.0, 1.0).astype(BF))
    wide_row = LANES // rb
    lane_f = jnp.bitwise_and(lane, wide_row - 1)
    own_row = lax.shift_right_logical(
        lax.broadcasted_iota(jnp.int32, (rb, LANES), 1), wide_row.bit_length() - 1
    ) == lax.broadcasted_iota(jnp.int32, (rb, LANES), 0)
    head_of = jnp.where(
        jnp.bitwise_and(lax.broadcasted_iota(jnp.int32, (LANES, cb), 0), wide_row - 1)
        == lax.shift_right_logical(lax.broadcasted_iota(jnp.int32, (LANES, cb), 1), 6),
        1.0, 0.0,
    )

    def flat(x):
        return jnp.sum(jnp.where(own_row, x, 0.0), axis=0, keepdims=True)

    def spread(x):
        rows = [jnp.where(own_row, x[i:i + 1], 0.0) for i in range(nc)]
        return jnp.dot(
            jnp.concatenate(rows, axis=0), head_of, preferred_element_type=F32,
            precision=lax.Precision.HIGHEST,
        )

    def stacked(x):
        return jnp.concatenate([x * m for m in halves], axis=0)

    def with_ones(x):
        return jnp.concatenate([x, jnp.ones(x.shape, BF)], axis=1)

    per = cb // LANES

    def global_scores(cg):
        for j in range(per):
            p = cg * per + j
            s = lax.dot_general(
                stacked(kv[glob0:glob0 + gblk, 2, p].reshape(NG, LANES)),
                kv[1:1 + nblk, 0, p].reshape(tok_dev, LANES), NT,
                preferred_element_type=F32,
            )
            gsc[cg % 2, j] = s
            gtop[cg % 2, j] = jnp.broadcast_to(
                jnp.max(s, axis=-1, keepdims=True), (2 * NG, LANES)
            )

    def global_sums(cg):
        nums, stat = [], jnp.zeros((NG, LANES), F32)
        for j in range(per):
            p = cg * per + j
            m = gtop[cg % 2, j]
            shift = jnp.concatenate([m] * (tok_dev // LANES), axis=1)
            e = jnp.exp2((gsc[cg % 2, j] - shift) * EXP_SCALE).astype(BF)
            x = jnp.dot(
                e, with_ones(kv[1:1 + nblk, 1, p].reshape(tok_dev, LANES)),
                preferred_element_type=F32,
            )
            nums.append(jnp.where(islo, x[:NG, :LANES], x[NG:, :LANES]).astype(BF))
            m = m * SCORE_SCALE
            for h in range(2):
                rows = slice(h * NG, (h + 1) * NG)
                stat = jnp.where(lane_f == 2 * j + h, m[rows], stat)
                stat = jnp.where(lane_f == hpb + 2 * j + h, x[rows, LANES:], stat)
        num = jnp.concatenate(nums, axis=1) if per > 1 else nums[0]
        for rg in range(NG // rb):
            d = rg * ncg + cg
            cn_out[d % 2, d // 2] = num[rg * rb:(rg + 1) * rb]
            cs_out[d % 2, d // 2] = flat(stat[rg * rb:(rg + 1) * rb])

    global_scores(0)
    for cg in range(ncg):
        global_sums(cg)
        if cg + 1 < ncg:
            global_scores(cg + 1)
    cs_mate.start()
    cn_mate.start()

    def merge_pair():
        cs_mate.wait_recv()
        cn_mate.wait_recv()
        a, b = cs_out[core].reshape(nc, LANES), cs_pair[...].reshape(nc, LANES)
        m = jnp.maximum(a, b)
        ea, eb = jnp.exp(a - m), jnp.exp(b - m)
        t = a * pltpu.roll(ea, hpb, 1) + b * pltpu.roll(eb, hpb, 1)
        cs_mid[...] = jnp.where(lane_f < hpb, m, t).reshape(nc, 1, LANES)
        clean = lane_f < hpb
        fa, fb = spread(jnp.where(clean, ea, 0.0)), spread(jnp.where(clean, eb, 0.0))
        for i in range(nc):
            rows = slice(i * rb, (i + 1) * rb)
            cn_mid[i] = (
                cn_out[core, i].astype(F32) * fa[rows] + cn_pair[i].astype(F32) * fb[rows]
            ).astype(BF)
        to_chips(lambda p: cs_mid.at[p], cs_in.at[chip], 2)
        to_chips(lambda p: cn_mid.at[p], cn_in.at[chip], 3)
        cs_in[chip] = cs_mid[chip]
        cn_in[chip] = cn_mid[chip]

    def choose(b):
        picks = []
        for r in range(RAND):
            rel = rb_ref[r, b] - me * nblk
            dev = lax.div(rel + FAR * nblk, nblk)
            slot = jnp.where(dev < FAR, dev, dev - 1)
            pick = jnp.where(dev == FAR, rel + 1, far0 + slot)
            picks.append(jnp.minimum(jnp.maximum(pick, 0), far0 + NFAR - 1))
        return picks

    def rows_of(which, p, b, picks):
        return jnp.concatenate(
            [kv[b + i, which, p] for i in range(3)]
            + [kv[i, which, p] for i in picks]
            + [kv[glob0 + i, which, p] for i in range(gblk)],
            axis=0,
        )

    half = pairs // 2
    nsub = (3 + RAND) * BLK // LANES + NG // LANES

    def wide(x):
        return jnp.concatenate([x] * nsub, axis=1)

    def scores(g, blk):
        t, b, picks, bias = blk
        for j in range(half):
            p = g * half + j
            s = lax.dot_general(
                stacked(kv[1 + b, 2, p]), rows_of(0, p, b, picks), NT, preferred_element_type=F32
            )
            if bias is not None:
                s = s + bias
            sc[g, j] = s
            top[g, j] = jnp.broadcast_to(
                jnp.max(s, axis=-1, keepdims=True), (2 * BLK, LANES)
            )

    def expo(g):
        for j in range(half):
            e = jnp.exp2((sc[g, j] - wide(top[g, j])) * EXP_SCALE)
            ex[g, j] = e
            inv[g, j] = jnp.broadcast_to(
                1.0 / jnp.sum(e, axis=-1, keepdims=True), (2 * BLK, LANES)
            )

    def weigh(g, blk):
        t, b, picks, _ = blk
        for j in range(0, half, 2):
            p = g * half + j
            w = jnp.concatenate(
                [(ex[g, j + i] * wide(inv[g, j + i])).astype(BF) for i in range(2)], axis=0
            )
            x = jnp.dot(
                w,
                jnp.concatenate([rows_of(1, p + i, b, picks) for i in range(2)], axis=1),
                preferred_element_type=F32,
            )
            for i in range(2):
                y = x[i * 2 * BLK:(i + 1) * 2 * BLK, i * LANES:(i + 1) * LANES]
                sp[t, p + i] = jnp.where(islo, y[:BLK], y[BLK:]).astype(BF)

    def attend(before, blocks):
        seq = [before] + blocks
        for i, blk in enumerate(blocks):
            expo(1)
            scores(0, blk)
            weigh(0, seq[i])
            expo(0)
            scores(1, blk)
            weigh(1, seq[i])

    def block_at(t, b, bias=None):
        return t, b, choose(b), bias

    def between():
        for side, o in ((0, 1), (1, -1)):
            @pl.when(exists(o))
            def _():
                halo_copy(side).wait_recv()
        for i, o in enumerate(OFFSETS):
            @pl.when(exists(o))
            def _():
                far_copy(i).wait_recv()
        def project_edges(i, carry):
            rows = land[...].reshape((2 + NFAR) * BLK, width)
            val = jnp.dot(rows, wall[i], preferred_element_type=F32).astype(BF)
            for p in range(pairs):
                x = val[:, p * LANES:(p + 1) * LANES].reshape(2 + NFAR, BLK, LANES)
                kv[0, i, p] = x[0]
                kv[right0:glob0, i, p] = x[1:]
            return carry

        lax.fori_loop(0, 2, project_edges, 0)

        wait_chips(cs_in, all_r.at[2])
        wait_chips(cn_in, all_r.at[3])
        stat = cs_in[...].reshape(nc, LANES)
        e = jnp.exp(stat - jnp.max(stat, axis=0, keepdims=True))
        den = jnp.sum(pltpu.roll(stat, LANES - hpb, 1) * e, axis=0, keepdims=True)
        fac = spread(jnp.where(lane_f < hpb, e / den, 0.0))
        num = cn_in[0].astype(F32) * fac[0:rb]
        for i in range(1, nc):
            num = num + cn_in[i].astype(F32) * fac[i * rb:(i + 1) * rb]
        ag2[core, chip] = num.astype(BF)
        to_chips(lambda p: ag2.at[core, chip], ag2.at[core, chip], 4)

    def two(i, carry):
        @pl.when(i == 1)
        def _():
            merge_pair()

        @pl.when(i == nblk // 4)
        def _():
            between()

        prev = jnp.maximum(2 * i - 1, 0)
        attend(
            block_at(prev, order[prev]),
            [block_at(2 * i + j, order[2 * i + j]) for j in range(2)],
        )
        return carry

    lax.fori_loop(0, nblk // 2 - 1, two, 0)
    wait_chips(ag2.at[0], all_r.at[4])
    ag2_mate.start()
    key_col = lax.broadcasted_iota(jnp.int32, (1, (3 + RAND) * BLK + NG), 1)
    lead = jnp.where(me == 0, BLK, 0)
    tail = jnp.where(me == n - 1, 2 * BLK, 3 * BLK)
    first = jnp.where(key_col < lead, -1e30, 0.0)
    last = jnp.where((key_col >= tail) & (key_col < 3 * BLK), -1e30, 0.0)
    end = block_at(nblk - 1, nblk - 1, last)
    attend(block_at(nblk - 3, order[nblk - 3]), [block_at(nblk - 2, 0, first), end])
    expo(1)
    weigh(0, end)
    weigh(1, end)

    ag2_mate.wait_recv()
    for d in range(n):
        r, c = (d // ncg) * rb, (d % ncg) * cb
        if rb % 16 == 0:
            gout[r:r + rb, c:c + cb] = ag2[d % 2, d // 2]
        else:
            gf[r:r + rb, c:c + cb] = ag2[d % 2, d // 2].astype(F32)
    if rb % 16:
        gout[...] = gf[...].astype(BF)

    for i, o in enumerate(OFFSETS):
        @pl.when(exists(o))
        def _():
            req_copy(i).wait_send()

        @pl.when(exists(-o))
        def _():
            far_copy(i).wait_send()
    for side, o in ((0, -1), (1, 1)):
        @pl.when(exists(o))
        def _():
            halo_copy(side).wait_send()
    for cp in (rs_mate, ag_mate, cs_mate, cn_mate, ag2_mate):
        cp.wait_send()
    for i, buf in enumerate((rs_mid, ag.at[0], cs_mid, cn_mid, ag2.at[0])):
        wait_chips(buf, all_s.at[i])


def mix(step, tok_dev, place, start_ref, sp, gout, grow_ref, wo, out_ref):
    c = pl.program_id(0)
    at = c * step
    pairs = sp.shape[1]
    pos = start_ref[0] + at + lax.broadcasted_iota(jnp.int32, (step, NG), 0)
    one = jnp.where(pos == grow_ref[...], 1.0, 0.0)
    is_g = jnp.max(one, axis=-1, keepdims=True) > 0.5
    put = jnp.dot(one.astype(BF), gout[...], preferred_element_type=F32)
    own = jnp.concatenate(
        [
            jnp.concatenate([sp[place[c * (step // BLK) + i], p] for p in range(pairs)], axis=1)
            for i in range(step // BLK)
        ],
        axis=0,
    )
    att = jnp.where(is_g, put, own.astype(F32)).astype(BF)
    out_ref[...] = jnp.dot(att, wo[...], preferred_element_type=F32).astype(BF)


def body(n, tokens, w_query, w_key, w_value, w_out, rand_blocks, global_pos):
    tok_dev, width = tokens.shape
    nblk = tok_dev // BLK
    pairs = width // LANES
    cb = 256 if n <= 32 else 128
    rb = NG * width // (n * cb)
    ext = nblk + 2 + NFAR + NG // BLK
    dma = pltpu.SemaphoreType.DMA
    vm = pltpu.VMEM
    nc = n // 2
    both = vm((2, nc, rb, cb), BF)
    piece = vm((nc, rb, cb), BF)
    stat = vm((nc, 1, LANES), F32)
    keys = (3 + RAND) * BLK + NG
    big = vm((2, pairs // 2, 2 * BLK, keys), F32)
    small = vm((2, pairs // 2, 2 * BLK, LANES), F32)
    scratch = [
        vm((nblk, BLK, width), BF), vm((3, width, width), BF),
        vm((ext, 3, pairs, BLK, LANES), BF),
        vm((NG, width), BF), vm((NG, width), F32), vm((NG, tok_dev), BF),
        vm((NFAR, BLK, width), BF), vm((2 + NFAR, BLK, width), BF),
        vm((NFAR, 8, LANES), jnp.int32), vm((NFAR, 8, LANES), jnp.int32),
        pltpu.SMEM((nblk,), jnp.int32),
        both, piece, piece, piece, both, both, piece, piece, piece,
        vm((2, nc, 1, LANES), F32), stat, stat, stat, both,
        big, small, big, small,
        vm((2, cb // LANES, 2 * NG, tok_dev), F32), vm((2, cb // LANES, 2 * NG, LANES), F32),
        dma((4,)), dma((NFAR,)), dma((NFAR,)), dma((2 + NFAR,)), dma((2 + NFAR,)),
        dma((5,)), dma((5,)), dma((5,)), dma((5,)),
    ]
    anyspace = pl.BlockSpec(memory_space=pl.ANY)
    vmem = pl.BlockSpec(memory_space=pltpu.VMEM)
    smem = pl.BlockSpec(memory_space=pltpu.SMEM)
    grow = global_pos.reshape(1, NG)
    rbt = rand_blocks.T
    sp, gout, place = pl.pallas_call(
        functools.partial(attention, n),
        out_shape=(
            jax.ShapeDtypeStruct((nblk, pairs, BLK, LANES), BF),
            jax.ShapeDtypeStruct((NG, width), BF),
            jax.ShapeDtypeStruct((nblk,), jnp.int32),
        ),
        in_specs=[anyspace] * 4 + [vmem] * 2 + [smem],
        out_specs=(vmem, vmem, smem),
        scratch_shapes=scratch,
        compiler_params=pltpu.CompilerParams(
            collective_id=0, has_side_effects=True, vmem_limit_bytes=51 << 20
        ),
        name="attention",
    )(tokens.reshape(nblk, BLK, width), w_query, w_key, w_value, rbt, grow, rbt)
    step = 512
    start = (lax.axis_index("seq") * tok_dev).reshape(1).astype(jnp.int32)
    return pl.pallas_call(
        functools.partial(mix, step, tok_dev),
        grid=(tok_dev // step,),
        out_shape=jax.ShapeDtypeStruct((tok_dev, width), BF),
        in_specs=[smem, smem, vmem, vmem, vmem, vmem],
        out_specs=pl.BlockSpec((step, width), lambda i: (i, 0)),
        compiler_params=pltpu.CompilerParams(vmem_limit_bytes=32 << 20),
        name="mix",
    )(place, start, sp, gout, grow, w_out)


def solution(mesh):
    placed = (P("seq", None), P(), P(), P(), P(), P("seq", None), P())
    return jax.shard_map(
        functools.partial(body, mesh.shape["seq"]), mesh=mesh, in_specs=placed,
        out_specs=P("seq", None), check_vma=False,
    )
```
